32 devices in a mesh: dp: 8 (over z, x), head: 4 (over y, core).
Axes of the slice: x: 2, y: 2, z: 4, core: 2. Of those that a mesh axis runs over, the one named last changes fastest.
Arguments:
- vit_ctx: bfloat16 [1024, 1536], P('dp', 'head'), may hold values from -6 to 6
- vit_resid: bfloat16 [1024, 1600], P('dp'), may hold values from -6 to 6
- vit_proj: bfloat16 [4, 384, 1600], P('head', 'dp'), may hold values from -0.15625 to 0.15625
- vit_grad: bfloat16 [1024, 1600], P('dp'), may hold values from -6 to 6
- norm_gain: float32 [1600], replicated, may hold values from 0.1 to 1.9
- cross_q: bfloat16 [96, 2048], P(None, 'head'), may hold values from -400 to 400
- key_w: bfloat16 [1600, 2048], P(None, 'head'), may hold values from -0.15625 to 0.15625
- value_w: bfloat16 [1600, 2048], P(None, 'head'), may hold values from -0.15625 to 0.15625
- out_w: bfloat16 [2048, 4096], P('head'), may hold values from -0.125 to 0.125
- query_state: bfloat16 [96, 4096], P(None, 'head'), may hold values from -1.5 to 1.5
Outputs:
- ctx_grad: bfloat16 [1024, 1536], P('dp', 'head')
- proj_grad: float32 [4, 384, 1600], P('head', 'dp')
- cross_out: bfloat16 [8, 96, 4096], P('dp', None, 'head')
The draws below stay inside these ranges and needn't reach their ends.
All inputs are finite; a program needn't handle non-finite values.
Results may differ from the reference program's by a relative error of at most 0.017.
The reference program's roundings to bfloat16 on the way count: a program that leaves them out, or rounds other values in their place, can miss the bound.
Values may be sent and summed in bfloat16 or wider, within the bound.
A program may use at most 64 MiB of HBM per device.

```python
import math
import jax
import jax.numpy as jnp
from jax import lax

D = 1600
HD = 128
QW = 4096
NQ = 96
TOK_DEV = 128
VROWS = 384
VCTX = 1536
CHEADS = 16
CW = 2048
VTOK = 1024
N_DP = 8
N_HEAD = 4


def draw_cross_q(key, part):
    base_key = jax.random.fold_in(jax.random.fold_in(key, 17), 0)
    values = jax.random.normal(base_key, (NQ, CHEADS * HD), jnp.float32)
    return jnp.clip(values, -400.0, 400.0).astype(jnp.bfloat16)


def levels(rng, shape, shards, smallest, high):
    gain, own = 1.0, jax.random.fold_in(rng, 6)
    for axis_at, parts in shards:
        steps = jnp.exp(jax.random.uniform(jax.random.fold_in(own, axis_at), (parts,), jnp.float32, smallest / len(shards), high / len(shards)))
        gain = gain * jnp.repeat(steps, shape[axis_at] // parts).reshape([-1 if axis == axis_at else 1 for axis in range(len(shape))])
    return gain


def noise(rng, dims, scale, most, pieces=(), kind=jnp.bfloat16):
    gain = levels(rng, dims, pieces, -0.22, 0.18) if pieces else 1.0
    values = jax.random.normal(rng, dims, jnp.float32) * scale * gain
    return jnp.minimum(jnp.maximum(values, -most), most).astype(kind)


def setup_inputs(seed: int = 0) -> dict:
    key_list = jax.random.split(jax.random.key(seed), 11)
    return {
        "vit_ctx": noise(key_list[0], (VTOK, VCTX), 1.0, 6.0, ((0, 8), (1, 4))),
        "vit_resid": noise(key_list[1], (VTOK, D), 1.0, 6.0, ((0, 8),)),
        "vit_proj": noise(key_list[2], (N_HEAD, VROWS, D), VCTX ** -0.5, 0.15625, ((0, 4), (1, 8))),
        "vit_grad": noise(key_list[3], (VTOK, D), 1.0, 6.0, ((0, 8),)),
        "norm_gain": jnp.clip(1.0 + 0.18 * jax.random.normal(key_list[4], (D,), jnp.float32), 0.1, 1.9),
        "cross_q": draw_cross_q(jax.random.fold_in(key_list[10], 71), 0),
        "key_w": noise(key_list[6], (D, CW), D ** -0.5, 0.15625, ((1, 4),)),
        "value_w": noise(key_list[7], (D, CW), D ** -0.5, 0.15625, ((1, 4),)),
        "out_w": noise(key_list[8], (CW, QW), CW ** -0.5, 0.125, ((0, 4),)),
        "query_state": noise(key_list[9], (NQ, QW), 0.25, 1.5, ((1, 4),)),
    }


EPSILON = 1e-06

def layer_norm(hidden, norm_gain):
    row_mean = lax.optimization_barrier(jnp.mean(hidden, axis=1, keepdims=True))
    square_mean = lax.optimization_barrier(jnp.mean(hidden * hidden, axis=1, keepdims=True))
    variance = square_mean - row_mean * row_mean
    return (hidden - row_mean) * lax.rsqrt(variance + EPSILON) * norm_gain

def reference(vit_ctx, vit_resid, vit_proj, vit_grad, norm_gain, cross_q, key_w, value_w, out_w, query_state):
    proj_matrix = vit_proj.reshape(VCTX, D)
    hidden = vit_resid.astype(jnp.float32) + jnp.dot(vit_ctx, proj_matrix, preferred_element_type=jnp.float32)
    features = layer_norm(hidden, norm_gain).astype(jnp.bfloat16)
    queries = cross_q.astype(jnp.float32).reshape(NQ, CHEADS, HD)

    def one_image(feats_image):
        key_rows = jnp.dot(feats_image, key_w, preferred_element_type=jnp.float32).astype(jnp.bfloat16)
        value_rows = jnp.dot(feats_image, value_w, preferred_element_type=jnp.float32).astype(jnp.bfloat16)
        key_heads = key_rows.astype(jnp.float32).reshape(TOK_DEV, CHEADS, HD)
        value_heads = value_rows.astype(jnp.float32).reshape(TOK_DEV, CHEADS, HD)
        scores = jnp.einsum('qhd,khd->hqk', queries, key_heads) * (1.0 / math.sqrt(HD))
        row_max = lax.optimization_barrier(jnp.max(scores, axis=2, keepdims=True))
        exponent = jnp.exp(scores - row_max)
        attn_probs = (exponent / lax.optimization_barrier(jnp.sum(exponent, axis=2, keepdims=True))).astype(jnp.bfloat16)
        attended = jnp.einsum('hqk,khd->qhd', attn_probs.astype(jnp.float32), value_heads)
        attended = attended.astype(jnp.bfloat16).reshape(NQ, CW)
        return (jnp.dot(attended, out_w, preferred_element_type=jnp.float32) + query_state.astype(jnp.float32)).astype(jnp.bfloat16)
    cross_out = lax.map(one_image, features.reshape(N_DP, TOK_DEV, D))
    ctx_grad = lax.dot_general(vit_grad, proj_matrix, (((1,), (1,)), ((), ())), preferred_element_type=jnp.float32).astype(jnp.bfloat16)
    proj_grad = lax.dot_general(vit_ctx, vit_grad, (((0,), (0,)), ((), ())), preferred_element_type=jnp.float32)
    return (ctx_grad, proj_grad.reshape(N_HEAD, VROWS, D), cross_out)
```

```python
import functools
import math
from types import SimpleNamespace

import jax
import jax.numpy as jnp
from jax import lax
from jax.experimental import pallas as pl
from jax.experimental.pallas import tpu as pltpu
from jax.sharding import PartitionSpec as P

HD = 128
EPSILON = 1e-06
MESH = pl.DeviceIdType.MESH
F32 = jnp.float32
BF16 = jnp.bfloat16


def peer_along(at, step, count):
    if count & (count - 1):
        return lax.rem(at + step, count)
    bit = 1
    while bit < count:
        if step & bit:
            at = at + bit - 2 * bit * lax.rem(at // bit, 2)
        bit *= 2
    return at


def named(tree):
    if isinstance(tree, dict):
        return SimpleNamespace(**{k: named(v) for k, v in tree.items()})
    return tree


def remote_in(sends):
    def remote(src, dst, sems, at, device):
        copy = pltpu.make_async_remote_copy(
            src_ref=src,
            dst_ref=dst,
            send_sem=sems[0].at[at],
            recv_sem=sems[1].at[at],
            device_id=device,
            device_id_type=MESH,
        )
        copy.start()
        sends.append(copy)
        return copy

    return remote


def attention(cross_q, keys, values):
    scale = 1.0 / math.sqrt(HD)
    attended = []
    for lo in range(0, keys.shape[1], HD):
        scores = (
            lax.dot_general(
                cross_q[:, lo : lo + HD],
                keys[:, lo : lo + HD],
                (((1,), (1,)), ((), ())),
                preferred_element_type=F32,
            )
            * scale
        )
        exponent = jnp.exp(scores - jnp.max(scores, axis=1, keepdims=True))
        probs = (exponent / jnp.sum(exponent, axis=1, keepdims=True)).astype(BF16)
        attended.append(
            jnp.dot(probs, values[:, lo : lo + HD], preferred_element_type=F32).astype(BF16)
        )
    return jnp.concatenate(attended, axis=1)


def paired_kernel(tree, n, spans, cuts, *refs):
    ins, outs, scratch = jax.tree.unflatten(tree, refs)
    r = named(ins | outs | scratch)
    sends = []
    remote = remote_in(sends)
    d, e = lax.axis_index("dp"), lax.axis_index("head")
    m = n // 2
    z, x = d // 2, lax.rem(d, 2)
    y, c = e // 2, lax.rem(e, 2)
    z_pos = [z] + [peer_along(z, k, m) for k in range(1, m)]
    z_peer = [(2 * p + x, e) for p in z_pos]
    x_peer, core_peer = (2 * z + 1 - x, e), (d, 2 * y + 1 - c)
    y_peer, across = (d, 2 * (1 - y) + c), (2 * z + 1 - x, 2 * (1 - y) + c)

    greet = [x_peer, core_peer, y_peer, across] + z_peer[1:]
    barrier = pltpu.get_barrier_semaphore()
    for device in greet:
        pl.semaphore_signal(barrier, inc=1, device_id=device, device_id_type=MESH)

    proj, gradt = r.src.proj, r.gradt
    rows, width = proj.shape
    tokens = r.v.ctx.shape[0]
    half = tokens // 2
    own, theirs = slice(0, tokens), slice(tokens, 2 * tokens)
    loads = [(r.src.ctx, r.v.ctx)]
    loads += [(proj.at[:, lo:hi], r.gath[i].at[z]) for i, (lo, hi) in enumerate(spans)]
    loads += [(r.src.grad, gradt.at[:, own])]
    streams = [k for k in vars(r.v) if k != "ctx"]
    loads += [(getattr(r.src, k), getattr(r.v, k)) for k in streams]
    loads = [pltpu.make_async_copy(*pair, r.load.at[at]) for at, pair in enumerate(loads)]
    for load in loads:
        load.start()
    first = loads[: 2 + len(spans)]
    waits = named(dict(zip(streams, loads[len(first) :])))

    first[0].wait()
    ctx_all, ctx_t = r.ctx_all, r.ctx_t
    ctx_all[...] = r.v.ctx[...].T.reshape(n, rows, tokens)
    for k in range(m):
        at = slice(k * rows, (k + 1) * rows)
        r.ctx_send[at] = ctx_all[2 * k + 1 - x]
        ctx_t[at, own] = ctx_all[2 * k + x]
    for load in first[1:]:
        load.wait()

    pl.semaphore_wait(barrier, len(greet))
    gather = {}
    to_ctx = remote(r.ctx_send, ctx_t.at[:, theirs], r.sems.ctx, 0, x_peer)
    for i in range(len(spans)):
        here = r.gath[i].at[z]
        for k in range(m - 1, 0, -1):
            gather[i, k] = remote(here, here, r.sems.ag[i], k - 1, z_peer[k])
    part = pl.ds(pl.multiple_of(c * (width // 2), 16), width // 2)
    to_grad = remote(gradt.at[part, own], gradt.at[part, theirs], r.sems.grad, 0, x_peer)

    own_rows = pl.ds(pl.multiple_of(c * half, half), half)
    peer_rows = pl.ds(pl.multiple_of((1 - c) * half, half), half)
    waits.resid.wait()
    resid = r.resid_n
    for lo in range(0, width, 128):
        hi = min(lo + 128, width)
        resid[:, lo:hi] = r.v.resid[lo:hi, :].T

    ctx_n, lhs = r.ctx_n, r.lhs
    to_ctx.wait_recv()
    for at, group in enumerate((own, theirs)):
        ctx_n[at] = ctx_t[:, group].T
        lhs[at * half : (at + 1) * half] = ctx_n[at, peer_rows]
        lhs[(2 + at) * half : (3 + at) * half] = ctx_n[at, own_rows]

    def matrix(i):
        lo, hi = spans[i]
        return r.gath[i][...].reshape(m * rows, hi - lo)

    to_core, to_x, to_y, to_across = {}, {}, {}, {}

    def product(i):
        for k in range(1, m):
            gather[i, k].wait_recv()
        hs = r.hs[i]
        hs[...] = jnp.dot(lhs[...], matrix(i), preferred_element_type=F32)
        to_core[i] = remote(hs.at[: 2 * half], r.crecv[i], r.sems.core[i], 0, core_peer)

    def exchange(i):
        hs, crecv, psend, precv = r.hs[i], r.crecv[i], r.psend[i], r.precv[i]
        to_core[i].wait_recv()
        psend[1] = (hs[3 * half :] + crecv[half:]).astype(BF16)
        to_across[i] = remote(psend.at[1], precv.at[2], r.sems.part[i], 2, across)
        to_x[i] = remote(psend.at[1], precv.at[1], r.sems.part[i], 1, x_peer)
        chip_sum = hs[2 * half : 3 * half] + crecv[:half]
        psend[0] = chip_sum.astype(BF16)
        to_y[i] = remote(psend.at[0], precv.at[0], r.sems.part[i], 0, y_peer)
        hs[2 * half : 3 * half] = chip_sum

    def pass_grad():
        to_grad.wait_recv()
        got = gradt.at[part, theirs]
        return remote(got, got, r.sems.grad, 1, core_peer)

    def weight_grad():
        dwf, zsend = r.dwf, r.zsend
        for lo in range(0, width, 256):
            hi = min(lo + 256, width)
            dwf[:, :, lo:hi] = lax.dot_general(
                ctx_t[...], gradt[lo:hi, :], (((1,), (1,)), ((), ())), preferred_element_type=F32
            ).reshape(m, rows, hi - lo)
        for k in range(1, m):
            zsend[k - 1] = dwf[z_pos[k]].astype(BF16)

    last = len(spans) - 1
    for i in range(last):
        product(i)
        exchange(i)
        if i == 0:
            to_grad2 = pass_grad()
        if i == last - 1:
            to_grad2.wait_recv()
            weight_grad()
    product(last)
    scatter = {
        k: remote(r.zsend.at[k - 1], r.zrecv.at[k - 1], r.sems.rs, k - 1, z_peer[k])
        for k in range(m - 1, 0, -1)
    }
    exchange(last)

    grads = 0.0
    for i, (lo, hi) in enumerate(spans):
        grads = grads + jnp.dot(matrix(i), gradt[lo:hi, :], preferred_element_type=F32)
    r.cg_own[...] = grads[:, own].astype(BF16).reshape(m, rows, tokens)
    r.cg_send[...] = grads[:, theirs].astype(BF16).reshape(m, rows, tokens)
    to_cg = remote(r.cg_send, r.cg_recv, r.sems.cg, 0, x_peer)

    feat = r.feat
    total, squares = 0.0, 0.0
    for i, (lo, hi) in enumerate(spans):
        precv, hs = r.precv[i], r.hs[i]
        hidden = resid[own_rows, lo:hi].astype(F32) + hs[2 * half : 3 * half]
        for at, copies in enumerate((to_y, to_x, to_across)):
            copies[i].wait_recv()
            hidden = hidden + precv[at].astype(F32)
        hs[2 * half : 3 * half] = hidden
        total = total + jnp.sum(hidden, axis=1, keepdims=True)
        squares = squares + jnp.sum(hidden * hidden, axis=1, keepdims=True)
    row_mean, square_mean = total / width, squares / width
    variance = square_mean - row_mean * row_mean
    inverse = lax.rsqrt(variance + EPSILON)
    waits.gain.wait()
    scales = r.v.gain[...].reshape(1, width)
    for i, (lo, hi) in enumerate(spans):
        feat[own_rows, lo:hi] = (
            (r.hs[i][2 * half : 3 * half] - row_mean) * inverse * scales[:, lo:hi]
        ).astype(BF16)
    to_feat = remote(feat.at[own_rows], feat.at[own_rows], r.sems.feat, 0, core_peer)
    for load in (waits.key_w, waits.value_w, waits.cross_q):
        load.wait()
    to_feat.wait_recv()

    keys = jnp.dot(feat[...], r.v.key_w[...], preferred_element_type=F32).astype(BF16)
    values = jnp.dot(feat[...], r.v.value_w[...], preferred_element_type=F32).astype(BF16)
    attended = attention(r.v.cross_q, keys, values)

    waits.out_w.wait()
    waits.query_state.wait()
    out_w, query_state = r.v.out_w, r.v.query_state
    wide = query_state.shape[1]

    def term(chip, core, lo, hi):
        at = pl.multiple_of((2 * chip + core) * wide + lo, 128)
        return jnp.dot(attended, out_w[:, pl.ds(at, hi - lo)], preferred_element_type=F32)

    osend, orecv, kept, o2send, o2recv = r.osend, r.orecv, r.kept, r.o2send, r.o2recv
    to_pair, to_out = {}, {}
    for k, chip in ((1, 1 - y), (0, y)):
        for j, (lo, hi) in enumerate(cuts):
            osend[k, :, lo:hi] = term(chip, 1 - c, lo, hi).astype(BF16)
            to_pair[k, j] = remote(
                osend.at[k, :, lo:hi], orecv.at[k, :, lo:hi], r.sems.pair, k * len(cuts) + j, core_peer
            )
        if k:
            for lo, hi in cuts:
                kept[k, :, lo:hi] = term(chip, c, lo, hi)
    for j, (lo, hi) in enumerate(cuts):
        to_pair[1, j].wait_recv()
        o2send[:, lo:hi] = (kept[1, :, lo:hi] + orecv[1, :, lo:hi].astype(F32)).astype(BF16)
        to_out[j] = remote(o2send.at[:, lo:hi], o2recv.at[:, lo:hi], r.sems.out, j, y_peer)
    for j, (lo, hi) in enumerate(cuts):
        to_pair[0, j].wait_recv()
        kept[0, :, lo:hi] = (
            query_state[:, lo:hi].astype(F32) + term(y, c, lo, hi) + orecv[0, :, lo:hi].astype(F32)
        )

    to_cg.wait_recv()
    cg_all = r.cg_all
    for k in range(m):
        cg_all[2 * k + x] = r.cg_own[k]
        cg_all[2 * k + 1 - x] = r.cg_recv[k]
    r.ctx_grad[...] = cg_all[...].reshape(n * rows, tokens).T

    total = r.dwf[z]
    for k in range(m - 1, 0, -1):
        scatter[k].wait_recv()
        total = total + r.zrecv[k - 1].astype(F32)
    r.proj_grad[...] = total

    for j, (lo, hi) in enumerate(cuts):
        to_out[j].wait_recv()
        r.cross_out[:, lo:hi] = (kept[0, :, lo:hi] + o2recv[:, lo:hi].astype(F32)).astype(BF16)

    for copy in sends:
        copy.wait_send()


def dma(count):
    return pltpu.SemaphoreType.DMA((max(count, 1),))


def pair(count):
    return dma(count), dma(count)


def call(kernel, sizes, ins, outs, scratch):
    specs, tree = jax.tree.flatten((ins, {k: k for k in outs}, scratch))
    args = jax.tree.leaves(ins)
    results = pl.pallas_call(
        functools.partial(kernel, tree, *sizes),
        out_shape=[jax.ShapeDtypeStruct(*v) for v in outs.values()],
        in_specs=[pl.BlockSpec(memory_space=pl.ANY)] * len(args),
        out_specs=[pl.BlockSpec(memory_space=pltpu.VMEM)] * len(outs),
        scratch_shapes=specs[len(args) + len(outs) :],
        compiler_params=pltpu.CompilerParams(collective_id=0, has_side_effects=True),
    )(*args)
    return hand_over(results)


def cut(width, parts):
    tiles, spans, at = -(-width // 128), [], 0
    for left in range(parts, 0, -1):
        take = -(-tiles // left) if left > 1 else tiles
        tiles -= take
        spans.append((at, min(at + take * 128, width)))
        at += take * 128
    return spans


def paired(n, vit_ctx, vit_resid, proj, vit_grad, norm_gain, cross_q, key_w, value_w, out_w, query_state):
    rows, width = proj.shape
    tokens, vrows = vit_ctx.shape
    queries, wide = query_state.shape
    m, half = n // 2, tokens // 2
    src = dict(
        proj=proj, ctx=vit_ctx, grad=vit_grad.T, resid=vit_resid.T, key_w=key_w, value_w=value_w,
        gain=norm_gain, cross_q=cross_q, query_state=query_state, out_w=out_w,
    )
    outs = dict(
        cross_out=((queries, wide), BF16), ctx_grad=((tokens, vrows), BF16), proj_grad=((rows, width), F32)
    )
    spans = cut(width, 4)
    cuts = cut(wide, 2)
    direct = dict(proj=proj, grad=vit_grad.T)
    scratch = dict(
        v={k: pltpu.VMEM(a.shape, a.dtype) for k, a in src.items() if k not in direct},
        load=dma(len(src) + len(spans)),
        gradt=pltpu.VMEM((width, 2 * tokens), BF16),
        ctx_all=pltpu.VMEM((n, rows, tokens), BF16),
        ctx_t=pltpu.VMEM((m * rows, 2 * tokens), BF16),
        ctx_send=pltpu.VMEM((m * rows, tokens), BF16),
        ctx_n=pltpu.VMEM((2, tokens, m * rows), BF16),
        lhs=pltpu.VMEM((2 * tokens, m * rows), BF16),
        resid_n=pltpu.VMEM((tokens, width), BF16),
        dwf=pltpu.VMEM((m, rows, width), F32),
        zsend=pltpu.VMEM((max(m - 1, 1), rows, width), BF16),
        zrecv=pltpu.VMEM((max(m - 1, 1), rows, width), BF16),
        cg_own=pltpu.VMEM((m, rows, tokens), BF16),
        cg_send=pltpu.VMEM((m, rows, tokens), BF16),
        cg_recv=pltpu.VMEM((m, rows, tokens), BF16),
        cg_all=pltpu.VMEM((n, rows, tokens), BF16),
        feat=pltpu.VMEM((tokens, width), BF16),
        osend=pltpu.VMEM((2, queries, wide), BF16),
        orecv=pltpu.VMEM((2, queries, wide), BF16),
        kept=pltpu.VMEM((2, queries, wide), F32),
        o2send=pltpu.VMEM((queries, wide), BF16),
        o2recv=pltpu.VMEM((queries, wide), BF16),
        gath=[pltpu.VMEM((m, rows, hi - lo), BF16) for lo, hi in spans],
        hs=[pltpu.VMEM((2 * tokens, hi - lo), F32) for lo, hi in spans],
        crecv=[pltpu.VMEM((tokens, hi - lo), F32) for lo, hi in spans],
        psend=[pltpu.VMEM((2, half, hi - lo), BF16) for lo, hi in spans],
        precv=[pltpu.VMEM((3, half, hi - lo), BF16) for lo, hi in spans],
        sems=dict(
            ctx=pair(1), grad=pair(2), rs=pair(m - 1), cg=pair(1), feat=pair(1), out=pair(len(cuts)),
            pair=pair(2 * len(cuts)), ag=[pair(m - 1) for _ in spans], core=[pair(1) for _ in spans],
            part=[pair(3) for _ in spans],
        ),
    )
    cross_out, ctx_grad, proj_grad = call(paired_kernel, (n, spans, cuts), dict(src=src), outs, scratch)
    return ctx_grad, cross_out, proj_grad


def spread_kernel(tree, h, spans, *refs):
    ins, outs, scratch = jax.tree.unflatten(tree, refs)
    r = named(ins | outs | scratch)
    sends = []
    remote = remote_in(sends)
    ctx, resid, grad, gain, cross_q, query_state = (
        r.v.ctx, r.v.resid, r.v.grad, r.v.gain, r.v.cross_q, r.v.query_state
    )
    proj = r.v.proj
    d, e = lax.axis_index("dp"), lax.axis_index("head")
    chips = h // 2
    y, c = e // 2, lax.rem(e, 2)
    core_peer = (d, 2 * y + 1 - c)
    y_pos = [y] + [lax.rem(y + k, chips) for k in range(1, chips)]
    y_peer = [(d, 2 * p + c) for p in y_pos]

    waits = {}
    for i, name in enumerate(vars(r.src)):
        waits[name] = pltpu.make_async_copy(getattr(r.src, name), getattr(r.v, name), r.load.at[i])
        waits[name].start()
    waits = named(waits)

    greet = [core_peer] + y_peer[1:]
    greeted = [core_peer] + [(d, 2 * lax.rem(y + chips - k, chips) + c) for k in range(1, chips)]
    barrier = pltpu.get_barrier_semaphore()
    for device in greeted:
        pl.semaphore_signal(barrier, inc=1, device_id=device, device_id_type=MESH)
    pl.semaphore_wait(barrier, len(greet))

    width = spans[-1][1]

    def flip(src, dst):
        for lo in range(0, width, 128):
            hi = min(lo + 128, width)
            dst[:, lo:hi] = src[lo:hi, :].T

    for load in (waits.ctx, waits.grad, waits.resid, waits.proj):
        load.wait()
    flip(grad, r.grad_n)
    flip(resid, r.resid_n)
    grad, resid = r.grad_n, r.resid_n

    half = ctx.shape[0] // 2
    own_rows = pl.ds(pl.multiple_of(c * half, half), half)
    peer_rows = pl.ds(pl.multiple_of((1 - c) * half, half), half)
    feat = r.feat
    to_core, to_y = {}, {}
    for i, (lo, hi) in enumerate(spans):
        hs, ysend, yrecv = r.hs[i], r.ysend[i], r.yrecv[i]
        hs[1] = jnp.dot(ctx[peer_rows, :], proj[:, lo:hi], preferred_element_type=F32)
        to_core[i] = remote(hs.at[1], r.crecv[i], r.sems.core[i], 0, core_peer)
        hs[0] = jnp.dot(ctx[own_rows, :], proj[:, lo:hi], preferred_element_type=F32)
        to_core[i].wait_recv()
        chip_sum = hs[0] + r.crecv[i][...]
        hs[0] = chip_sum
        ysend[...] = chip_sum.astype(BF16)
        for k in range(1, chips):
            to_y[i, k] = remote(ysend, yrecv.at[k - 1], r.sems.y[i], k - 1, y_peer[k])

    grads = 0.0
    for i, (lo, hi) in enumerate(spans):
        grads = grads + lax.dot_general(
            grad[:, lo:hi], proj[:, lo:hi], (((1,), (1,)), ((), ())), preferred_element_type=F32
        )
    r.ctx_grad[...] = grads.astype(BF16)

    total, squares = 0.0, 0.0
    for i, (lo, hi) in enumerate(spans):
        hidden = resid[own_rows, lo:hi].astype(F32) + r.hs[i][0]
        for k in range(1, chips):
            to_y[i, k].wait_recv()
            hidden = hidden + r.yrecv[i][k - 1].astype(F32)
        r.hs[i][0] = hidden
        total = total + jnp.sum(hidden, axis=1, keepdims=True)
        squares = squares + jnp.sum(hidden * hidden, axis=1, keepdims=True)
    row_mean, square_mean = total / width, squares / width
    variance = square_mean - row_mean * row_mean
    inverse = lax.rsqrt(variance + EPSILON)
    waits.gain.wait()
    scales = gain[...].reshape(1, width)
    for i, (lo, hi) in enumerate(spans):
        feat[own_rows, lo:hi] = (
            (r.hs[i][0] - row_mean) * inverse * scales[:, lo:hi]
        ).astype(BF16)
    to_feat = remote(feat.at[own_rows], feat.at[own_rows], r.sems.feat, 0, core_peer)
    for load in (waits.key_w, waits.value_w, waits.cross_q):
        load.wait()
    to_feat.wait_recv()

    keys = jnp.dot(feat[...], r.v.key_w[...], preferred_element_type=F32).astype(BF16)
    values = jnp.dot(feat[...], r.v.value_w[...], preferred_element_type=F32).astype(BF16)
    attended = attention(cross_q, keys, values)

    waits.out_w.wait()
    waits.query_state.wait()
    out_w, wide = r.v.out_w, query_state.shape[1]

    def term(chip, core):
        at = pl.multiple_of((2 * chip + core) * wide, 128)
        return jnp.dot(attended, out_w[:, pl.ds(at, wide)], preferred_element_type=F32)

    osend, orecv, kept = r.osend, r.orecv, r.kept
    to_pair, to_out = {}, {}
    for k in list(range(1, chips)) + [0]:
        osend[k] = term(y_pos[k], 1 - c).astype(BF16)
        to_pair[k] = remote(osend.at[k], orecv.at[k], r.sems.pair, k, core_peer)
        kept[k] = term(y_pos[k], c)
        if k:
            to_pair[k].wait_recv()
            r.o2send[k - 1] = (kept[k] + orecv[k].astype(F32)).astype(BF16)
            to_out[k] = remote(r.o2send.at[k - 1], r.o2recv.at[k - 1], r.sems.out, k - 1, y_peer[k])

    to_pair[0].wait_recv()
    result = query_state[...].astype(F32) + kept[0] + orecv[0].astype(F32)
    for k in range(1, chips):
        to_out[k].wait_recv()
        result = result + r.o2recv[k - 1].astype(F32)
    r.cross_out[...] = result.astype(BF16)

    for copy in sends:
        copy.wait_send()


def spread(h, vit_ctx, vit_resid, vit_proj, vit_grad, norm_gain, cross_q, key_w, value_w, out_w, query_state):
    tokens, vrows = vit_ctx.shape
    queries, wide = query_state.shape
    width = vit_proj.shape[2]
    chips, half = h // 2, tokens // 2
    src = dict(
        proj=lax.all_gather(vit_proj, "dp", axis=1, tiled=True)[0], ctx=vit_ctx, grad=vit_grad.T, resid=vit_resid.T,
        key_w=key_w, value_w=value_w, gain=norm_gain, cross_q=cross_q, query_state=query_state, out_w=out_w,
    )
    outs = dict(cross_out=((queries, wide), BF16), ctx_grad=((tokens, vrows), BF16))
    spans = cut(width, 2)
    ahead = max(chips - 1, 1)
    scratch = dict(
        v={k: pltpu.VMEM(a.shape, a.dtype) for k, a in src.items()},
        load=dma(len(src)),
        grad_n=pltpu.VMEM((tokens, width), BF16),
        resid_n=pltpu.VMEM((tokens, width), BF16),
        feat=pltpu.VMEM((tokens, width), BF16),
        osend=pltpu.VMEM((chips, queries, wide), BF16),
        orecv=pltpu.VMEM((chips, queries, wide), BF16),
        kept=pltpu.VMEM((chips, queries, wide), F32),
        o2send=pltpu.VMEM((ahead, queries, wide), BF16),
        o2recv=pltpu.VMEM((ahead, queries, wide), BF16),
        hs=[pltpu.VMEM((2, half, hi - lo), F32) for lo, hi in spans],
        crecv=[pltpu.VMEM((half, hi - lo), F32) for lo, hi in spans],
        ysend=[pltpu.VMEM((half, hi - lo), BF16) for lo, hi in spans],
        yrecv=[pltpu.VMEM((ahead, half, hi - lo), BF16) for lo, hi in spans],
        sems=dict(
            feat=pair(1), pair=pair(chips), out=pair(chips - 1), core=[pair(1) for _ in spans],
            y=[pair(chips - 1) for _ in spans],
        ),
    )
    cross_out, ctx_grad = call(spread_kernel, (h, spans), dict(src=src), outs, scratch)
    proj_grad = lax.psum_scatter(
        lax.dot_general(vit_ctx, vit_grad, (((0,), (0,)), ((), ())), preferred_element_type=F32),
        "dp", scatter_dimension=0, tiled=True,
    )
    return ctx_grad, cross_out, proj_grad


def hand_over_kernel(*refs):
    count = len(refs) // 2
    for src, dst in zip(refs[:count], refs[count:]):
        dst[...] = src[...]


def hand_over(results):
    vmem = pl.BlockSpec(memory_space=pltpu.VMEM)
    return pl.pallas_call(
        hand_over_kernel,
        out_shape=[jax.ShapeDtypeStruct(a.shape, a.dtype) for a in results],
        in_specs=[vmem] * len(results),
        out_specs=[vmem] * len(results),
    )(*results)


def on_device(
    n, h, vit_ctx, vit_resid, vit_proj, vit_grad, norm_gain, cross_q, key_w, value_w, out_w, query_state
):
    rest = vit_grad, norm_gain, cross_q, key_w, value_w, out_w, query_state
    rows, width = vit_proj.shape[1:]
    if h == 4 and n % 2 == 0 and rows % 16 == 0 and width % 32 == 0:
        ctx_grad, cross_out, proj_grad = paired(n, vit_ctx, vit_resid, vit_proj[0], *rest)
    else:
        ctx_grad, cross_out, proj_grad = spread(h, vit_ctx, vit_resid, vit_proj, *rest)
    return ctx_grad, proj_grad[None], cross_out[None]


def solution(mesh):
    return jax.shard_map(
        functools.partial(on_device, mesh.shape["dp"], mesh.shape["head"]),
        mesh=mesh,
        in_specs=(
            P("dp", "head"),
            P("dp", None),
            P("head", "dp", None),
            P("dp", None),
            P(),
            P(None, "head"),
            P(None, "head"),
            P(None, "head"),
            P("head", None),
            P(None, "head"),
        ),
        out_specs=(P("dp", "head"), P("head", "dp", None), P("dp", None, "head")),
        check_vma=False,
    )
```

```python
import functools
import math
from types import SimpleNamespace

import jax
import jax.numpy as jnp
from jax import lax
from jax.experimental import pallas as pl
from jax.experimental.pallas import tpu as pltpu
from jax.sharding import PartitionSpec as P

HD = 128
EPSILON = 1e-06
MESH = pl.DeviceIdType.MESH
F32 = jnp.float32
BF16 = jnp.bfloat16


def named(tree):
    if isinstance(tree, dict):
        return SimpleNamespace(**{k: named(v) for k, v in tree.items()})
    return tree


def remote_in(sends):
    def remote(src, dst, sems, at, device):
        copy = pltpu.make_async_remote_copy(
            src_ref=src,
            dst_ref=dst,
            send_sem=sems[0].at[at],
            recv_sem=sems[1].at[at],
            device_id=device,
            device_id_type=MESH,
        )
        copy.start()
        sends.append(copy)
        return copy

    return remote


def attention(cross_q, keys, values):
    scale = 1.0 / math.sqrt(HD)
    attended = []
    for lo in range(0, keys.shape[1], HD):
        scores = (
            lax.dot_general(
                cross_q[:, lo : lo + HD],
                keys[:, lo : lo + HD],
                (((1,), (1,)), ((), ())),
                preferred_element_type=F32,
            )
            * scale
        )
        exponent = jnp.exp(scores - jnp.max(scores, axis=1, keepdims=True))
        probs = (exponent / jnp.sum(exponent, axis=1, keepdims=True)).astype(BF16)
        attended.append(
            jnp.dot(probs, values[:, lo : lo + HD], preferred_element_type=F32).astype(BF16)
        )
    return jnp.concatenate(attended, axis=1)


def paired_kernel(tree, n, spans, cuts, *refs):
    ins, outs, scratch = jax.tree.unflatten(tree, refs)
    r = named(ins | outs | scratch)
    sends = []
    remote = remote_in(sends)
    d, e = lax.axis_index("dp"), lax.axis_index("head")
    m = n // 2
    z, x = d // 2, lax.rem(d, 2)
    y, c = e // 2, lax.rem(e, 2)
    z_near, z_far = z + 1 - 2 * lax.rem(z, 2), lax.rem(z + 2, m)
    z_last = m - 1 - z
    near, far = (2 * z_near + x, e), (2 * z_far + x, e)
    x_peer, core_peer = (2 * z + 1 - x, e), (d, 2 * y + 1 - c)
    y_peer, across = (d, 2 * (1 - y) + c), (2 * z + 1 - x, 2 * (1 - y) + c)

    greet = [x_peer, core_peer, y_peer, across, near, far]
    barrier = pltpu.get_barrier_semaphore()
    for device in greet:
        pl.semaphore_signal(barrier, inc=1, device_id=device, device_id_type=MESH)

    proj, gradt = r.src.proj, r.gradt
    rows, width = proj.shape
    tokens = r.v.ctx.shape[0]
    half = tokens // 2
    own, theirs = slice(0, tokens), slice(tokens, 2 * tokens)
    loads = [(r.src.ctx, r.v.ctx)]
    loads += [(proj.at[:, lo:hi], r.gath[i].at[z]) for i, (lo, hi) in enumerate(spans)]
    loads += [(r.src.grad, gradt.at[:, own])]
    streams = [k for k in vars(r.v) if k != "ctx"]
    loads += [(getattr(r.src, k), getattr(r.v, k)) for k in streams]
    loads = [pltpu.make_async_copy(*pair, r.load.at[at]) for at, pair in enumerate(loads)]
    for load in loads:
        load.start()
    first = loads[: 2 + len(spans)]
    waits = named(dict(zip(streams, loads[len(first) :])))

    first[0].wait()
    ctx_all, ctx_t = r.ctx_all, r.ctx_t
    ctx_all[...] = r.v.ctx[...].T.reshape(n, rows, tokens)
    for k in range(m):
        at = slice(k * rows, (k + 1) * rows)
        r.ctx_send[at] = ctx_all[2 * k + 1 - x]
        ctx_t[at, own] = ctx_all[2 * k + x]
    for load in first[1:]:
        load.wait()

    pl.semaphore_wait(barrier, len(greet))
    gather = {}
    to_ctx = remote(r.ctx_send, ctx_t.at[:, theirs], r.sems.ctx, 0, x_peer)
    for k, device in enumerate((far, near)):
        for i in range(len(spans)):
            here = r.gath[i].at[z]
            gather[i, k] = remote(here, here, r.sems.ag[i], k, device)
    part = pl.ds(pl.multiple_of(c * (width // 2), 16), width // 2)
    to_grad = remote(gradt.at[part, own], gradt.at[part, theirs], r.sems.grad, 0, x_peer)

    own_rows = pl.ds(pl.multiple_of(c * half, half), half)
    peer_rows = pl.ds(pl.multiple_of((1 - c) * half, half), half)
    waits.resid.wait()
    resid = r.resid_n
    for lo in range(0, width, 128):
        hi = min(lo + 128, width)
        resid[:, lo:hi] = r.v.resid[lo:hi, :].T

    ctx_n, lhs = r.ctx_n, r.lhs
    to_ctx.wait_recv()
    for at, group in enumerate((own, theirs)):
        ctx_n[at] = ctx_t[:, group].T
        lhs[at * half : (at + 1) * half] = ctx_n[at, peer_rows]
        lhs[(2 + at) * half : (3 + at) * half] = ctx_n[at, own_rows]

    def matrix(i):
        lo, hi = spans[i]
        return r.gath[i][...].reshape(m * rows, hi - lo)

    to_core, to_x, to_y, to_across = {}, {}, {}, {}

    def forward(i):
        gather[i, 0].wait_recv()
        here = r.gath[i].at[z_far]
        gather[i, 2] = remote(here, here, r.sems.ag[i], 2, near)

    def product(i):
        gather[i, 1].wait_recv()
        gather[i, 2].wait_recv()
        hs = r.hs[i]
        hs[...] = jnp.dot(lhs[...], matrix(i), preferred_element_type=F32)
        to_core[i] = remote(hs.at[: 2 * half], r.crecv[i], r.sems.core[i], 0, core_peer)

    def exchange(i):
        hs, crecv, psend, precv = r.hs[i], r.crecv[i], r.psend[i], r.precv[i]
        to_core[i].wait_recv()
        psend[1] = (hs[3 * half :] + crecv[half:]).astype(BF16)
        to_across[i] = remote(psend.at[1], precv.at[2], r.sems.part[i], 2, across)
        to_x[i] = remote(psend.at[1], precv.at[1], r.sems.part[i], 1, x_peer)
        chip_sum = hs[2 * half : 3 * half] + crecv[:half]
        psend[0] = chip_sum.astype(BF16)
        to_y[i] = remote(psend.at[0], precv.at[0], r.sems.part[i], 0, y_peer)
        hs[2 * half : 3 * half] = chip_sum

    def pass_grad():
        to_grad.wait_recv()
        got = gradt.at[part, theirs]
        return remote(got, got, r.sems.grad, 1, core_peer)

    def weight_grad():
        dwf, zsend = r.dwf, r.zsend
        for lo in range(0, width, 256):
            hi = min(lo + 256, width)
            dwf[:, :, lo:hi] = lax.dot_general(
                ctx_t[...], gradt[lo:hi, :], (((1,), (1,)), ((), ())), preferred_element_type=F32
            ).reshape(m, rows, hi - lo)
        for k, block in enumerate((z_last, z_near)):
            zsend[k] = dwf[block].astype(BF16)

    def pass_weight_grad():
        to_near[0].wait_recv()
        r.zsend[2] = (r.dwf[z_far] + r.zrecv[0].astype(F32)).astype(BF16)
        return remote(r.zsend.at[2], r.zrecv.at[2], r.sems.rs, 2, far)

    last = len(spans) - 1
    forward(0)
    for i in range(last):
        forward(i + 1)
        product(i)
        exchange(i)
        if i == 0:
            to_grad2 = pass_grad()
        if i == last - 1:
            to_grad2.wait_recv()
            weight_grad()
    product(last)
    to_near = [remote(r.zsend.at[k], r.zrecv.at[k], r.sems.rs, k, near) for k in range(2)]
    exchange(last)

    grads = 0.0
    for i, (lo, hi) in enumerate(spans):
        grads = grads + jnp.dot(matrix(i), gradt[lo:hi, :], preferred_element_type=F32)
    r.cg_own[...] = grads[:, own].astype(BF16).reshape(m, rows, tokens)
    r.cg_send[...] = grads[:, theirs].astype(BF16).reshape(m, rows, tokens)
    to_cg = remote(r.cg_send, r.cg_recv, r.sems.cg, 0, x_peer)

    feat = r.feat
    total, squares = 0.0, 0.0
    for i, (lo, hi) in enumerate(spans):
        precv, hs = r.precv[i], r.hs[i]
        hidden = resid[own_rows, lo:hi].astype(F32) + hs[2 * half : 3 * half]
        for at, copies in enumerate((to_y, to_x, to_across)):
            copies[i].wait_recv()
            hidden = hidden + precv[at].astype(F32)
        hs[2 * half : 3 * half] = hidden
        total = total + jnp.sum(hidden, axis=1, keepdims=True)
        squares = squares + jnp.sum(hidden * hidden, axis=1, keepdims=True)
    row_mean, square_mean = total / width, squares / width
    variance = square_mean - row_mean * row_mean
    inverse = lax.rsqrt(variance + EPSILON)
    waits.gain.wait()
    scales = r.v.gain[...].reshape(1, width)
    for i, (lo, hi) in enumerate(spans):
        feat[own_rows, lo:hi] = (
            (r.hs[i][2 * half : 3 * half] - row_mean) * inverse * scales[:, lo:hi]
        ).astype(BF16)
    to_feat = remote(feat.at[own_rows], feat.at[own_rows], r.sems.feat, 0, core_peer)
    for load in (waits.key_w, waits.value_w, waits.cross_q):
        load.wait()
    to_feat.wait_recv()
    to_far = pass_weight_grad()

    keys = jnp.dot(feat[...], r.v.key_w[...], preferred_element_type=F32).astype(BF16)
    values = jnp.dot(feat[...], r.v.value_w[...], preferred_element_type=F32).astype(BF16)
    attended = attention(r.v.cross_q, keys, values)

    waits.out_w.wait()
    waits.query_state.wait()
    out_w, query_state = r.v.out_w, r.v.query_state
    wide = query_state.shape[1]

    def term(chip, core, lo, hi):
        at = pl.multiple_of((2 * chip + core) * wide + lo, 128)
        return jnp.dot(attended, out_w[:, pl.ds(at, hi - lo)], preferred_element_type=F32)

    osend, orecv, kept, o2send, o2recv = r.osend, r.orecv, r.kept, r.o2send, r.o2recv
    to_pair, to_out = {}, {}
    for k, chip in ((1, 1 - y), (0, y)):
        for j, (lo, hi) in enumerate(cuts):
            osend[k, :, lo:hi] = term(chip, 1 - c, lo, hi).astype(BF16)
            to_pair[k, j] = remote(
                osend.at[k, :, lo:hi], orecv.at[k, :, lo:hi], r.sems.pair, k * len(cuts) + j, core_peer
            )
        if k:
            for lo, hi in cuts:
                kept[k, :, lo:hi] = term(chip, c, lo, hi)
    for j, (lo, hi) in enumerate(cuts):
        to_pair[1, j].wait_recv()
        o2send[:, lo:hi] = (kept[1, :, lo:hi] + orecv[1, :, lo:hi].astype(F32)).astype(BF16)
        to_out[j] = remote(o2send.at[:, lo:hi], o2recv.at[:, lo:hi], r.sems.out, j, y_peer)
    for j, (lo, hi) in enumerate(cuts):
        to_pair[0, j].wait_recv()
        kept[0, :, lo:hi] = (
            query_state[:, lo:hi].astype(F32) + term(y, c, lo, hi) + orecv[0, :, lo:hi].astype(F32)
        )

    to_cg.wait_recv()
    cg_all = r.cg_all
    for k in range(m):
        cg_all[2 * k + x] = r.cg_own[k]
        cg_all[2 * k + 1 - x] = r.cg_recv[k]
    r.ctx_grad[...] = cg_all[...].reshape(n * rows, tokens).T

    total = r.dwf[z]
    for copy, k in ((to_near[1], 1), (to_far, 2)):
        copy.wait_recv()
        total = total + r.zrecv[k].astype(F32)
    r.proj_grad[...] = total

    for j, (lo, hi) in enumerate(cuts):
        to_out[j].wait_recv()
        r.cross_out[:, lo:hi] = (kept[0, :, lo:hi] + o2recv[:, lo:hi].astype(F32)).astype(BF16)

    for copy in sends:
        copy.wait_send()


def dma(count):
    return pltpu.SemaphoreType.DMA((max(count, 1),))


def pair(count):
    return dma(count), dma(count)


def call(kernel, sizes, ins, outs, scratch):
    specs, tree = jax.tree.flatten((ins, {k: k for k in outs}, scratch))
    args = jax.tree.leaves(ins)
    results = pl.pallas_call(
        functools.partial(kernel, tree, *sizes),
        out_shape=[jax.ShapeDtypeStruct(*v) for v in outs.values()],
        in_specs=[pl.BlockSpec(memory_space=pl.ANY)] * len(args),
        out_specs=[pl.BlockSpec(memory_space=pltpu.VMEM)] * len(outs),
        scratch_shapes=specs[len(args) + len(outs) :],
        compiler_params=pltpu.CompilerParams(collective_id=0, has_side_effects=True),
    )(*args)
    return hand_over(results)


def cut(width, parts):
    tiles, spans, at = -(-width // 128), [], 0
    for left in range(parts, 0, -1):
        take = -(-tiles // left) if left > 1 else tiles
        tiles -= take
        spans.append((at, min(at + take * 128, width)))
        at += take * 128
    return spans


def paired(n, vit_ctx, vit_resid, proj, vit_grad, norm_gain, cross_q, key_w, value_w, out_w, query_state):
    rows, width = proj.shape
    tokens, vrows = vit_ctx.shape
    queries, wide = query_state.shape
    m, half = n // 2, tokens // 2
    src = dict(
        proj=proj, ctx=vit_ctx, grad=vit_grad.T, resid=vit_resid.T, key_w=key_w, value_w=value_w,
        gain=norm_gain, cross_q=cross_q, query_state=query_state, out_w=out_w,
    )
    outs = dict(
        cross_out=((queries, wide), BF16), ctx_grad=((tokens, vrows), BF16), proj_grad=((rows, width), F32)
    )
    spans = cut(width, 4)
    cuts = cut(wide, 2)
    direct = dict(proj=proj, grad=vit_grad.T)
    scratch = dict(
        v={k: pltpu.VMEM(a.shape, a.dtype) for k, a in src.items() if k not in direct},
        load=dma(len(src) + len(spans)),
        gradt=pltpu.VMEM((width, 2 * tokens), BF16),
        ctx_all=pltpu.VMEM((n, rows, tokens), BF16),
        ctx_t=pltpu.VMEM((m * rows, 2 * tokens), BF16),
        ctx_send=pltpu.VMEM((m * rows, tokens), BF16),
        ctx_n=pltpu.VMEM((2, tokens, m * rows), BF16),
        lhs=pltpu.VMEM((2 * tokens, m * rows), BF16),
        resid_n=pltpu.VMEM((tokens, width), BF16),
        dwf=pltpu.VMEM((m, rows, width), F32),
        zsend=pltpu.VMEM((m - 1, rows, width), BF16),
        zrecv=pltpu.VMEM((m - 1, rows, width), BF16),
        cg_own=pltpu.VMEM((m, rows, tokens), BF16),
        cg_send=pltpu.VMEM((m, rows, tokens), BF16),
        cg_recv=pltpu.VMEM((m, rows, tokens), BF16),
        cg_all=pltpu.VMEM((n, rows, tokens), BF16),
        feat=pltpu.VMEM((tokens, width), BF16),
        osend=pltpu.VMEM((2, queries, wide), BF16),
        orecv=pltpu.VMEM((2, queries, wide), BF16),
        kept=pltpu.VMEM((2, queries, wide), F32),
        o2send=pltpu.VMEM((queries, wide), BF16),
        o2recv=pltpu.VMEM((queries, wide), BF16),
        gath=[pltpu.VMEM((m, rows, hi - lo), BF16) for lo, hi in spans],
        hs=[pltpu.VMEM((2 * tokens, hi - lo), F32) for lo, hi in spans],
        crecv=[pltpu.VMEM((tokens, hi - lo), F32) for lo, hi in spans],
        psend=[pltpu.VMEM((2, half, hi - lo), BF16) for lo, hi in spans],
        precv=[pltpu.VMEM((3, half, hi - lo), BF16) for lo, hi in spans],
        sems=dict(
            ctx=pair(1), grad=pair(2), rs=pair(m - 1), cg=pair(1), feat=pair(1), out=pair(len(cuts)),
            pair=pair(2 * len(cuts)), ag=[pair(m - 1) for _ in spans], core=[pair(1) for _ in spans],
            part=[pair(3) for _ in spans],
        ),
    )
    cross_out, ctx_grad, proj_grad = call(paired_kernel, (n, spans, cuts), dict(src=src), outs, scratch)
    return ctx_grad, cross_out, proj_grad


def spread_kernel(tree, h, spans, *refs):
    ins, outs, scratch = jax.tree.unflatten(tree, refs)
    r = named(ins | outs | scratch)
    sends = []
    remote = remote_in(sends)
    ctx, resid, grad, gain, cross_q, query_state = (
        r.v.ctx, r.v.resid, r.v.grad, r.v.gain, r.v.cross_q, r.v.query_state
    )
    proj = r.v.proj
    d, e = lax.axis_index("dp"), lax.axis_index("head")
    chips = h // 2
    y, c = e // 2, lax.rem(e, 2)
    core_peer = (d, 2 * y + 1 - c)
    y_pos = [y] + [lax.rem(y + k, chips) for k in range(1, chips)]
    y_peer = [(d, 2 * p + c) for p in y_pos]

    waits = {}
    for i, name in enumerate(vars(r.src)):
        waits[name] = pltpu.make_async_copy(getattr(r.src, name), getattr(r.v, name), r.load.at[i])
        waits[name].start()
    waits = named(waits)

    greet = [core_peer] + y_peer[1:]
    greeted = [core_peer] + [(d, 2 * lax.rem(y + chips - k, chips) + c) for k in range(1, chips)]
    barrier = pltpu.get_barrier_semaphore()
    for device in greeted:
        pl.semaphore_signal(barrier, inc=1, device_id=device, device_id_type=MESH)
    pl.semaphore_wait(barrier, len(greet))

    width = spans[-1][1]

    def flip(src, dst):
        for lo in range(0, width, 128):
            hi = min(lo + 128, width)
            dst[:, lo:hi] = src[lo:hi, :].T

    for load in (waits.ctx, waits.grad, waits.resid, waits.proj):
        load.wait()
    flip(grad, r.grad_n)
    flip(resid, r.resid_n)
    grad, resid = r.grad_n, r.resid_n

    half = ctx.shape[0] // 2
    own_rows = pl.ds(pl.multiple_of(c * half, half), half)
    peer_rows = pl.ds(pl.multiple_of((1 - c) * half, half), half)
    feat = r.feat
    to_core, to_y = {}, {}
    for i, (lo, hi) in enumerate(spans):
        hs, ysend, yrecv = r.hs[i], r.ysend[i], r.yrecv[i]
        hs[1] = jnp.dot(ctx[peer_rows, :], proj[:, lo:hi], preferred_element_type=F32)
        to_core[i] = remote(hs.at[1], r.crecv[i], r.sems.core[i], 0, core_peer)
        hs[0] = jnp.dot(ctx[own_rows, :], proj[:, lo:hi], preferred_element_type=F32)
        to_core[i].wait_recv()
        chip_sum = hs[0] + r.crecv[i][...]
        hs[0] = chip_sum
        ysend[...] = chip_sum.astype(BF16)
        for k in range(1, chips):
            to_y[i, k] = remote(ysend, yrecv.at[k - 1], r.sems.y[i], k - 1, y_peer[k])

    grads = 0.0
    for i, (lo, hi) in enumerate(spans):
        grads = grads + lax.dot_general(
            grad[:, lo:hi], proj[:, lo:hi], (((1,), (1,)), ((), ())), preferred_element_type=F32
        )
    r.ctx_grad[...] = grads.astype(BF16)

    total, squares = 0.0, 0.0
    for i, (lo, hi) in enumerate(spans):
        hidden = resid[own_rows, lo:hi].astype(F32) + r.hs[i][0]
        for k in range(1, chips):
            to_y[i, k].wait_recv()
            hidden = hidden + r.yrecv[i][k - 1].astype(F32)
        r.hs[i][0] = hidden
        total = total + jnp.sum(hidden, axis=1, keepdims=True)
        squares = squares + jnp.sum(hidden * hidden, axis=1, keepdims=True)
    row_mean, square_mean = total / width, squares / width
    variance = square_mean - row_mean * row_mean
    inverse = lax.rsqrt(variance + EPSILON)
    waits.gain.wait()
    scales = gain[...].reshape(1, width)
    for i, (lo, hi) in enumerate(spans):
        feat[own_rows, lo:hi] = (
            (r.hs[i][0] - row_mean) * inverse * scales[:, lo:hi]
        ).astype(BF16)
    to_feat = remote(feat.at[own_rows], feat.at[own_rows], r.sems.feat, 0, core_peer)
    for load in (waits.key_w, waits.value_w, waits.cross_q):
        load.wait()
    to_feat.wait_recv()

    keys = jnp.dot(feat[...], r.v.key_w[...], preferred_element_type=F32).astype(BF16)
    values = jnp.dot(feat[...], r.v.value_w[...], preferred_element_type=F32).astype(BF16)
    attended = attention(cross_q, keys, values)

    waits.out_w.wait()
    waits.query_state.wait()
    out_w, wide = r.v.out_w, query_state.shape[1]

    def term(chip, core):
        at = pl.multiple_of((2 * chip + core) * wide, 128)
        return jnp.dot(attended, out_w[:, pl.ds(at, wide)], preferred_element_type=F32)

    osend, orecv, kept = r.osend, r.orecv, r.kept
    to_pair, to_out = {}, {}
    for k in list(range(1, chips)) + [0]:
        osend[k] = term(y_pos[k], 1 - c).astype(BF16)
        to_pair[k] = remote(osend.at[k], orecv.at[k], r.sems.pair, k, core_peer)
        kept[k] = term(y_pos[k], c)
        if k:
            to_pair[k].wait_recv()
            r.o2send[k - 1] = (kept[k] + orecv[k].astype(F32)).astype(BF16)
            to_out[k] = remote(r.o2send.at[k - 1], r.o2recv.at[k - 1], r.sems.out, k - 1, y_peer[k])

    to_pair[0].wait_recv()
    result = query_state[...].astype(F32) + kept[0] + orecv[0].astype(F32)
    for k in range(1, chips):
        to_out[k].wait_recv()
        result = result + r.o2recv[k - 1].astype(F32)
    r.cross_out[...] = result.astype(BF16)

    for copy in sends:
        copy.wait_send()


def spread(h, vit_ctx, vit_resid, vit_proj, vit_grad, norm_gain, cross_q, key_w, value_w, out_w, query_state):
    tokens, vrows = vit_ctx.shape
    queries, wide = query_state.shape
    width = vit_proj.shape[2]
    chips, half = h // 2, tokens // 2
    src = dict(
        proj=lax.all_gather(vit_proj, "dp", axis=1, tiled=True)[0], ctx=vit_ctx, grad=vit_grad.T, resid=vit_resid.T,
        key_w=key_w, value_w=value_w, gain=norm_gain, cross_q=cross_q, query_state=query_state, out_w=out_w,
    )
    outs = dict(cross_out=((queries, wide), BF16), ctx_grad=((tokens, vrows), BF16))
    spans = cut(width, 2)
    ahead = max(chips - 1, 1)
    scratch = dict(
        v={k: pltpu.VMEM(a.shape, a.dtype) for k, a in src.items()},
        load=dma(len(src)),
        grad_n=pltpu.VMEM((tokens, width), BF16),
        resid_n=pltpu.VMEM((tokens, width), BF16),
        feat=pltpu.VMEM((tokens, width), BF16),
        osend=pltpu.VMEM((chips, queries, wide), BF16),
        orecv=pltpu.VMEM((chips, queries, wide), BF16),
        kept=pltpu.VMEM((chips, queries, wide), F32),
        o2send=pltpu.VMEM((ahead, queries, wide), BF16),
        o2recv=pltpu.VMEM((ahead, queries, wide), BF16),
        hs=[pltpu.VMEM((2, half, hi - lo), F32) for lo, hi in spans],
        crecv=[pltpu.VMEM((half, hi - lo), F32) for lo, hi in spans],
        ysend=[pltpu.VMEM((half, hi - lo), BF16) for lo, hi in spans],
        yrecv=[pltpu.VMEM((ahead, half, hi - lo), BF16) for lo, hi in spans],
        sems=dict(
            feat=pair(1), pair=pair(chips), out=pair(chips - 1), core=[pair(1) for _ in spans],
            y=[pair(chips - 1) for _ in spans],
        ),
    )
    cross_out, ctx_grad = call(spread_kernel, (h, spans), dict(src=src), outs, scratch)
    proj_grad = lax.psum_scatter(
        lax.dot_general(vit_ctx, vit_grad, (((0,), (0,)), ((), ())), preferred_element_type=F32),
        "dp", scatter_dimension=0, tiled=True,
    )
    return ctx_grad, cross_out, proj_grad


def hand_over_kernel(*refs):
    count = len(refs) // 2
    for src, dst in zip(refs[:count], refs[count:]):
        dst[...] = src[...]


def hand_over(results):
    vmem = pl.BlockSpec(memory_space=pltpu.VMEM)
    return pl.pallas_call(
        hand_over_kernel,
        out_shape=[jax.ShapeDtypeStruct(a.shape, a.dtype) for a in results],
        in_specs=[vmem] * len(results),
        out_specs=[vmem] * len(results),
    )(*results)


def on_device(
    n, h, vit_ctx, vit_resid, vit_proj, vit_grad, norm_gain, cross_q, key_w, value_w, out_w, query_state
):
    rest = vit_grad, norm_gain, cross_q, key_w, value_w, out_w, query_state
    rows, width = vit_proj.shape[1:]
    if h == 4 and n == 8 and rows % 16 == 0 and width % 32 == 0:
        ctx_grad, cross_out, proj_grad = paired(n, vit_ctx, vit_resid, vit_proj[0], *rest)
    else:
        ctx_grad, cross_out, proj_grad = spread(h, vit_ctx, vit_resid, vit_proj, *rest)
    return ctx_grad, proj_grad[None], cross_out[None]


def solution(mesh):
    return jax.shard_map(
        functools.partial(on_device, mesh.shape["dp"], mesh.shape["head"]),
        mesh=mesh,
        in_specs=(
            P("dp", "head"),
            P("dp", None),
            P("head", "dp", None),
            P("dp", None),
            P(),
            P(None, "head"),
            P(None, "head"),
            P(None, "head"),
            P("head", None),
            P(None, "head"),
        ),
        out_specs=(P("dp", "head"), P("head", "dp", None), P("dp", None, "head")),
        check_vma=False,
    )
```

```python
import functools
import math
from types import SimpleNamespace

import jax
import jax.numpy as jnp
from jax import lax
from jax.experimental import pallas as pl
from jax.experimental.pallas import tpu as pltpu
from jax.sharding import PartitionSpec as P

HD = 128
EPSILON = 1e-06
MESH = pl.DeviceIdType.MESH
F32 = jnp.float32
BF16 = jnp.bfloat16


def named(tree):
    if isinstance(tree, dict):
        return SimpleNamespace(**{k: named(v) for k, v in tree.items()})
    return tree


def remote_in(sends):
    def remote(src, dst, sems, at, device):
        copy = pltpu.make_async_remote_copy(
            src_ref=src,
            dst_ref=dst,
            send_sem=sems[0].at[at],
            recv_sem=sems[1].at[at],
            device_id=device,
            device_id_type=MESH,
        )
        copy.start()
        sends.append(copy)
        return copy

    return remote


def attention(cross_q, keys, values):
    scale = 1.0 / math.sqrt(HD)
    attended = []
    for lo in range(0, keys.shape[1], HD):
        scores = (
            lax.dot_general(
                cross_q[:, lo : lo + HD],
                keys[:, lo : lo + HD],
                (((1,), (1,)), ((), ())),
                preferred_element_type=F32,
            )
            * scale
        )
        exponent = jnp.exp(scores - jnp.max(scores, axis=1, keepdims=True))
        probs = (exponent / jnp.sum(exponent, axis=1, keepdims=True)).astype(BF16)
        attended.append(
            jnp.dot(probs, values[:, lo : lo + HD], preferred_element_type=F32).astype(BF16)
        )
    return jnp.concatenate(attended, axis=1)


def paired_kernel(tree, n, spans, cuts, *refs):
    ins, outs, scratch = jax.tree.unflatten(tree, refs)
    r = named(ins | outs | scratch)
    sends = []
    remote = remote_in(sends)
    d, e = lax.axis_index("dp"), lax.axis_index("head")
    m = n // 2
    z, x = d // 2, lax.rem(d, 2)
    y, c = e // 2, lax.rem(e, 2)
    z_near, z_far = z + 1 - 2 * lax.rem(z, 2), lax.rem(z + 2, m)
    z_last = m - 1 - z
    near, far = (2 * z_near + x, e), (2 * z_far + x, e)
    x_peer, core_peer = (2 * z + 1 - x, e), (d, 2 * y + 1 - c)
    y_peer = (d, 2 * (1 - y) + c)

    greet = [x_peer, core_peer, y_peer, near, far]
    barrier = pltpu.get_barrier_semaphore()
    for device in greet:
        pl.semaphore_signal(barrier, inc=1, device_id=device, device_id_type=MESH)

    proj, gradt = r.src.proj, r.gradt
    rows, width = proj.shape
    tokens = r.v.ctx.shape[0]
    half = tokens // 2
    own, theirs = slice(0, tokens), slice(tokens, 2 * tokens)
    loads = [(r.src.ctx, r.v.ctx)]
    loads += [(proj.at[:, lo:hi], r.gath[i].at[z]) for i, (lo, hi) in enumerate(spans)]
    loads += [(r.src.grad, gradt.at[:, own])]
    streams = [k for k in vars(r.v) if k != "ctx"]
    loads += [(getattr(r.src, k), getattr(r.v, k)) for k in streams]
    loads = [pltpu.make_async_copy(*pair, r.load.at[at]) for at, pair in enumerate(loads)]
    for load in loads:
        load.start()
    first = loads[: 2 + len(spans)]
    waits = named(dict(zip(streams, loads[len(first) :])))

    first[0].wait()
    ctx_all, ctx_t = r.ctx_all, r.ctx_t
    ctx_all[...] = r.v.ctx[...].T.reshape(n, rows, tokens)
    for k in range(m):
        at = slice(k * rows, (k + 1) * rows)
        r.ctx_send[at] = ctx_all[2 * k + 1 - x]
        ctx_t[at, own] = ctx_all[2 * k + x]
    for load in first[1:]:
        load.wait()

    pl.semaphore_wait(barrier, len(greet))
    gather = {}
    to_ctx = remote(r.ctx_send, ctx_t.at[:, theirs], r.sems.ctx, 0, x_peer)

    def gather_own(i):
        here = r.gath[i].at[z]
        for k, device in enumerate((far, near)):
            gather[i, k] = remote(here, here, r.sems.ag[i], k, device)

    ahead, waited = 2, []
    for i in range(len(spans)):
        if i >= ahead:
            gather[i - ahead, 0].wait_send()
            waited.append(gather[i - ahead, 0])
        gather_own(i)
        if i == 0:
            part = pl.ds(pl.multiple_of(c * (width // 2), 16), width // 2)
            to_grad = remote(gradt.at[part, own], gradt.at[part, theirs], r.sems.grad, 0, x_peer)

    own_rows = pl.ds(pl.multiple_of(c * half, half), half)
    peer_rows = pl.ds(pl.multiple_of((1 - c) * half, half), half)
    waits.resid.wait()
    resid = r.resid_n
    for lo in range(0, width, 128):
        hi = min(lo + 128, width)
        resid[:, lo:hi] = r.v.resid[lo:hi, :].T

    ctx_n, lhs = r.ctx_n, r.lhs
    to_ctx.wait_recv()
    for at, group in enumerate((own, theirs)):
        ctx_n[at] = ctx_t[:, group].T
        lhs[at * half : (at + 1) * half] = ctx_n[at, peer_rows]
        lhs[(2 + at) * half : (3 + at) * half] = ctx_n[at, own_rows]

    def matrix(i):
        lo, hi = spans[i]
        return r.gath[i][...].reshape(m * rows, hi - lo)

    to_core, to_x, to_y = {}, {}, {}

    def forward(i):
        gather[i, 0].wait_recv()
        here = r.gath[i].at[z_far]
        gather[i, 2] = remote(here, here, r.sems.ag[i], 2, near)

    def product(i):
        gather[i, 1].wait_recv()
        gather[i, 2].wait_recv()
        hs = r.hs[i]
        hs[...] = jnp.dot(lhs[...], matrix(i), preferred_element_type=F32)
        to_core[i] = remote(hs.at[: 2 * half], r.crecv[i], r.sems.core[i], 0, core_peer)

    def exchange(i):
        hs, crecv, psend, precv = r.hs[i], r.crecv[i], r.psend[i], r.precv[i]
        to_core[i].wait_recv()
        if i in y_first:
            chip_sums = hs[2 * half :] + crecv[...]
            hs[2 * half :] = chip_sums
            psend[:2] = chip_sums.astype(BF16).reshape(2, half, hs.shape[1])
            to_y[i] = remote(psend.at[:2], precv.at[:2], r.sems.part[i], 0, y_peer)
            return
        psend[1] = (hs[3 * half :] + crecv[half:]).astype(BF16)
        to_x[i] = remote(psend.at[1], precv.at[1], r.sems.part[i], 1, x_peer)
        chip_sum = hs[2 * half : 3 * half] + crecv[:half]
        hs[2 * half : 3 * half] = chip_sum

    def pass_pair_sum(i):
        hs, psend, precv = r.hs[i], r.psend[i], r.precv[i]
        if i in y_first:
            to_y[i].wait_recv()
            psend[2] = (hs[3 * half :] + precv[1].astype(F32)).astype(BF16)
            to_x[i] = remote(psend.at[2], precv.at[2], r.sems.part[i], 1, x_peer)
            hs[2 * half : 3 * half] = hs[2 * half : 3 * half] + precv[0].astype(F32)
            return
        to_x[i].wait_recv()
        pair_sum = hs[2 * half : 3 * half] + precv[1].astype(F32)
        hs[2 * half : 3 * half] = pair_sum
        psend[0] = pair_sum.astype(BF16)
        to_y[i] = remote(psend.at[0], precv.at[0], r.sems.part[i], 0, y_peer)

    def pass_grad():
        to_grad.wait_recv()
        got = gradt.at[part, theirs]
        return remote(got, got, r.sems.grad, 1, core_peer)

    def weight_grad():
        dwf, zsend = r.dwf, r.zsend
        for lo in range(0, width, 256):
            hi = min(lo + 256, width)
            dwf[:, :, lo:hi] = lax.dot_general(
                ctx_t[...], gradt[lo:hi, :], (((1,), (1,)), ((), ())), preferred_element_type=F32
            ).reshape(m, rows, hi - lo)
        for k, block in enumerate((z_last, z_near)):
            zsend[k] = dwf[block].astype(BF16)

    def pass_weight_grad():
        to_near[0].wait_recv()
        r.zsend[2] = (r.dwf[z_far] + r.zrecv[0].astype(F32)).astype(BF16)
        return remote(r.zsend.at[2], r.zrecv.at[2], r.sems.rs, 2, far)

    last = len(spans) - 1
    y_first = (1,)
    for i in range(last + 1):
        forward(i)
    to_grad2 = pass_grad()
    to_grad2.wait_recv()
    weight_grad()
    for i in range(last + 1):
        product(i)
        if i:
            exchange(i - 1)
    to_near = [remote(r.zsend.at[0], r.zrecv.at[0], r.sems.rs, 0, near)]
    exchange(last)
    for i in range(last + 1):
        pass_pair_sum(i)

    grads = 0.0
    for i, (lo, hi) in enumerate(spans):
        grads = grads + jnp.dot(matrix(i), gradt[lo:hi, :], preferred_element_type=F32)
    r.cg_own[...] = grads[:, own].astype(BF16).reshape(m, rows, tokens)
    r.cg_send[...] = grads[:, theirs].astype(BF16).reshape(m, rows, tokens)
    to_cg = remote(r.cg_send, r.cg_recv, r.sems.cg, 0, x_peer)

    to_far = pass_weight_grad()
    to_near.append(remote(r.zsend.at[1], r.zrecv.at[1], r.sems.rs, 1, near))

    feat = r.feat
    total, squares = 0.0, 0.0
    for i, (lo, hi) in enumerate(spans):
        precv, hs = r.precv[i], r.hs[i]
        hidden = resid[own_rows, lo:hi].astype(F32) + hs[2 * half : 3 * half]
        copy, at = (to_x[i], 2) if i in y_first else (to_y[i], 0)
        copy.wait_recv()
        hidden = hidden + precv[at].astype(F32)
        hs[2 * half : 3 * half] = hidden
        total = total + jnp.sum(hidden, axis=1, keepdims=True)
        squares = squares + jnp.sum(hidden * hidden, axis=1, keepdims=True)
    row_mean, square_mean = total / width, squares / width
    variance = square_mean - row_mean * row_mean
    inverse = lax.rsqrt(variance + EPSILON)
    waits.gain.wait()
    scales = r.v.gain[...].reshape(1, width)
    for i, (lo, hi) in enumerate(spans):
        feat[own_rows, lo:hi] = (
            (r.hs[i][2 * half : 3 * half] - row_mean) * inverse * scales[:, lo:hi]
        ).astype(BF16)
    to_feat = remote(feat.at[own_rows], feat.at[own_rows], r.sems.feat, 0, core_peer)
    for load in (waits.key_w, waits.value_w, waits.cross_q):
        load.wait()
    to_feat.wait_recv()

    keys = jnp.dot(feat[...], r.v.key_w[...], preferred_element_type=F32).astype(BF16)
    values = jnp.dot(feat[...], r.v.value_w[...], preferred_element_type=F32).astype(BF16)
    attended = attention(r.v.cross_q, keys, values)

    waits.out_w.wait()
    waits.query_state.wait()
    out_w, query_state = r.v.out_w, r.v.query_state
    wide = query_state.shape[1]

    def term(chip, core, lo, hi):
        at = pl.multiple_of((2 * chip + core) * wide + lo, 128)
        return jnp.dot(attended, out_w[:, pl.ds(at, hi - lo)], preferred_element_type=F32)

    osend, orecv, kept, o2send, o2recv = r.osend, r.orecv, r.kept, r.o2send, r.o2recv
    to_pair, to_out = {}, {}
    for k, chip in ((1, 1 - y), (0, y)):
        for j, (lo, hi) in enumerate(cuts):
            osend[k, :, lo:hi] = term(chip, 1 - c, lo, hi).astype(BF16)
            to_pair[k, j] = remote(
                osend.at[k, :, lo:hi], orecv.at[k, :, lo:hi], r.sems.pair, k * len(cuts) + j, core_peer
            )
        if k:
            for lo, hi in cuts:
                kept[k, :, lo:hi] = term(chip, c, lo, hi)
    for j, (lo, hi) in enumerate(cuts):
        to_pair[1, j].wait_recv()
        o2send[:, lo:hi] = (kept[1, :, lo:hi] + orecv[1, :, lo:hi].astype(F32)).astype(BF16)
        to_out[j] = remote(o2send.at[:, lo:hi], o2recv.at[:, lo:hi], r.sems.out, j, y_peer)
    for j, (lo, hi) in enumerate(cuts):
        to_pair[0, j].wait_recv()
        kept[0, :, lo:hi] = (
            query_state[:, lo:hi].astype(F32) + term(y, c, lo, hi) + orecv[0, :, lo:hi].astype(F32)
        )

    to_cg.wait_recv()
    cg_all = r.cg_all
    for k in range(m):
        cg_all[2 * k + x] = r.cg_own[k]
        cg_all[2 * k + 1 - x] = r.cg_recv[k]
    r.ctx_grad[...] = cg_all[...].reshape(n * rows, tokens).T

    total = r.dwf[z]
    for copy, k in ((to_near[1], 1), (to_far, 2)):
        copy.wait_recv()
        total = total + r.zrecv[k].astype(F32)
    r.proj_grad[...] = total

    for j, (lo, hi) in enumerate(cuts):
        to_out[j].wait_recv()
        r.cross_out[:, lo:hi] = (kept[0, :, lo:hi] + o2recv[:, lo:hi].astype(F32)).astype(BF16)

    for copy in sends:
        if not any(copy is done for done in waited):
            copy.wait_send()


def dma(count):
    return pltpu.SemaphoreType.DMA((max(count, 1),))


def pair(count):
    return dma(count), dma(count)


def call(kernel, sizes, ins, outs, scratch):
    specs, tree = jax.tree.flatten((ins, {k: k for k in outs}, scratch))
    args = jax.tree.leaves(ins)
    results = pl.pallas_call(
        functools.partial(kernel, tree, *sizes),
        out_shape=[pltpu.VMEM(*v) for v in outs.values()],
        in_specs=[pl.BlockSpec(memory_space=pl.ANY)] * len(args),
        out_specs=[pl.BlockSpec(memory_space=pltpu.VMEM)] * len(outs),
        scratch_shapes=specs[len(args) + len(outs) :],
        compiler_params=pltpu.CompilerParams(collective_id=0, has_side_effects=True),
    )(*args)
    return hand_over(results)


def cut(width, parts):
    tiles, spans, at = -(-width // 128), [], 0
    for left in range(parts, 0, -1):
        take = -(-tiles // left) if left > 1 else tiles
        tiles -= take
        spans.append((at, min(at + take * 128, width)))
        at += take * 128
    return spans


def paired(n, vit_ctx, vit_resid, proj, vit_grad, norm_gain, cross_q, key_w, value_w, out_w, query_state):
    rows, width = proj.shape
    tokens, vrows = vit_ctx.shape
    queries, wide = query_state.shape
    m, half = n // 2, tokens // 2
    src = dict(
        proj=proj, ctx=vit_ctx, grad=vit_grad.T, resid=vit_resid.T, key_w=key_w, value_w=value_w,
        gain=norm_gain, cross_q=cross_q, query_state=query_state, out_w=out_w,
    )
    outs = dict(
        cross_out=((queries, wide), BF16), ctx_grad=((tokens, vrows), BF16), proj_grad=((rows, width), F32)
    )
    spans = cut(width, 4)
    cuts = cut(wide, 1)
    direct = dict(proj=proj, grad=vit_grad.T)
    scratch = dict(
        v={k: pltpu.VMEM(a.shape, a.dtype) for k, a in src.items() if k not in direct},
        load=dma(len(src) + len(spans)),
        gradt=pltpu.VMEM((width, 2 * tokens), BF16),
        ctx_all=pltpu.VMEM((n, rows, tokens), BF16),
        ctx_t=pltpu.VMEM((m * rows, 2 * tokens), BF16),
        ctx_send=pltpu.VMEM((m * rows, tokens), BF16),
        ctx_n=pltpu.VMEM((2, tokens, m * rows), BF16),
        lhs=pltpu.VMEM((2 * tokens, m * rows), BF16),
        resid_n=pltpu.VMEM((tokens, width), BF16),
        dwf=pltpu.VMEM((m, rows, width), F32),
        zsend=pltpu.VMEM((m - 1, rows, width), BF16),
        zrecv=pltpu.VMEM((m - 1, rows, width), BF16),
        cg_own=pltpu.VMEM((m, rows, tokens), BF16),
        cg_send=pltpu.VMEM((m, rows, tokens), BF16),
        cg_recv=pltpu.VMEM((m, rows, tokens), BF16),
        cg_all=pltpu.VMEM((n, rows, tokens), BF16),
        feat=pltpu.VMEM((tokens, width), BF16),
        osend=pltpu.VMEM((2, queries, wide), BF16),
        orecv=pltpu.VMEM((2, queries, wide), BF16),
        kept=pltpu.VMEM((2, queries, wide), F32),
        o2send=pltpu.VMEM((queries, wide), BF16),
        o2recv=pltpu.VMEM((queries, wide), BF16),
        gath=[pltpu.VMEM((m, rows, hi - lo), BF16) for lo, hi in spans],
        hs=[pltpu.VMEM((2 * tokens, hi - lo), F32) for lo, hi in spans],
        crecv=[pltpu.VMEM((tokens, hi - lo), F32) for lo, hi in spans],
        psend=[pltpu.VMEM((3, half, hi - lo), BF16) for lo, hi in spans],
        precv=[pltpu.VMEM((3, half, hi - lo), BF16) for lo, hi in spans],
        sems=dict(
            ctx=pair(1), grad=pair(2), rs=pair(m - 1), cg=pair(1), feat=pair(1), out=pair(len(cuts)),
            pair=pair(2 * len(cuts)), ag=[pair(m - 1) for _ in spans], core=[pair(1) for _ in spans],
            part=[pair(2) for _ in spans],
        ),
    )
    cross_out, ctx_grad, proj_grad = call(paired_kernel, (n, spans, cuts), dict(src=src), outs, scratch)
    return ctx_grad, cross_out, proj_grad


def spread_kernel(tree, h, spans, *refs):
    ins, outs, scratch = jax.tree.unflatten(tree, refs)
    r = named(ins | outs | scratch)
    sends = []
    remote = remote_in(sends)
    ctx, resid, grad, gain, cross_q, query_state = (
        r.v.ctx, r.v.resid, r.v.grad, r.v.gain, r.v.cross_q, r.v.query_state
    )
    proj = r.v.proj
    d, e = lax.axis_index("dp"), lax.axis_index("head")
    chips = h // 2
    y, c = e // 2, lax.rem(e, 2)
    core_peer = (d, 2 * y + 1 - c)
    y_pos = [y] + [lax.rem(y + k, chips) for k in range(1, chips)]
    y_peer = [(d, 2 * p + c) for p in y_pos]

    waits = {}
    for i, name in enumerate(vars(r.src)):
        waits[name] = pltpu.make_async_copy(getattr(r.src, name), getattr(r.v, name), r.load.at[i])
        waits[name].start()
    waits = named(waits)

    greet = [core_peer] + y_peer[1:]
    greeted = [core_peer] + [(d, 2 * lax.rem(y + chips - k, chips) + c) for k in range(1, chips)]
    barrier = pltpu.get_barrier_semaphore()
    for device in greeted:
        pl.semaphore_signal(barrier, inc=1, device_id=device, device_id_type=MESH)
    pl.semaphore_wait(barrier, len(greet))

    width = spans[-1][1]

    def flip(src, dst):
        for lo in range(0, width, 128):
            hi = min(lo + 128, width)
            dst[:, lo:hi] = src[lo:hi, :].T

    for load in (waits.ctx, waits.grad, waits.resid, waits.proj):
        load.wait()
    flip(grad, r.grad_n)
    flip(resid, r.resid_n)
    grad, resid = r.grad_n, r.resid_n

    half = ctx.shape[0] // 2
    own_rows = pl.ds(pl.multiple_of(c * half, half), half)
    peer_rows = pl.ds(pl.multiple_of((1 - c) * half, half), half)
    feat = r.feat
    to_core, to_y = {}, {}
    for i, (lo, hi) in enumerate(spans):
        hs, ysend, yrecv = r.hs[i], r.ysend[i], r.yrecv[i]
        hs[1] = jnp.dot(ctx[peer_rows, :], proj[:, lo:hi], preferred_element_type=F32)
        to_core[i] = remote(hs.at[1], r.crecv[i], r.sems.core[i], 0, core_peer)
        hs[0] = jnp.dot(ctx[own_rows, :], proj[:, lo:hi], preferred_element_type=F32)
        to_core[i].wait_recv()
        chip_sum = hs[0] + r.crecv[i][...]
        hs[0] = chip_sum
        ysend[...] = chip_sum.astype(BF16)
        for k in range(1, chips):
            to_y[i, k] = remote(ysend, yrecv.at[k - 1], r.sems.y[i], k - 1, y_peer[k])

    grads = 0.0
    for i, (lo, hi) in enumerate(spans):
        grads = grads + lax.dot_general(
            grad[:, lo:hi], proj[:, lo:hi], (((1,), (1,)), ((), ())), preferred_element_type=F32
        )
    r.ctx_grad[...] = grads.astype(BF16)

    total, squares = 0.0, 0.0
    for i, (lo, hi) in enumerate(spans):
        hidden = resid[own_rows, lo:hi].astype(F32) + r.hs[i][0]
        for k in range(1, chips):
            to_y[i, k].wait_recv()
            hidden = hidden + r.yrecv[i][k - 1].astype(F32)
        r.hs[i][0] = hidden
        total = total + jnp.sum(hidden, axis=1, keepdims=True)
        squares = squares + jnp.sum(hidden * hidden, axis=1, keepdims=True)
    row_mean, square_mean = total / width, squares / width
    variance = square_mean - row_mean * row_mean
    inverse = lax.rsqrt(variance + EPSILON)
    waits.gain.wait()
    scales = gain[...].reshape(1, width)
    for i, (lo, hi) in enumerate(spans):
        feat[own_rows, lo:hi] = (
            (r.hs[i][0] - row_mean) * inverse * scales[:, lo:hi]
        ).astype(BF16)
    to_feat = remote(feat.at[own_rows], feat.at[own_rows], r.sems.feat, 0, core_peer)
    for load in (waits.key_w, waits.value_w, waits.cross_q):
        load.wait()
    to_feat.wait_recv()

    keys = jnp.dot(feat[...], r.v.key_w[...], preferred_element_type=F32).astype(BF16)
    values = jnp.dot(feat[...], r.v.value_w[...], preferred_element_type=F32).astype(BF16)
    attended = attention(cross_q, keys, values)

    waits.out_w.wait()
    waits.query_state.wait()
    out_w, wide = r.v.out_w, query_state.shape[1]

    def term(chip, core):
        at = pl.multiple_of((2 * chip + core) * wide, 128)
        return jnp.dot(attended, out_w[:, pl.ds(at, wide)], preferred_element_type=F32)

    osend, orecv, kept = r.osend, r.orecv, r.kept
    to_pair, to_out = {}, {}
    for k in list(range(1, chips)) + [0]:
        osend[k] = term(y_pos[k], 1 - c).astype(BF16)
        to_pair[k] = remote(osend.at[k], orecv.at[k], r.sems.pair, k, core_peer)
        kept[k] = term(y_pos[k], c)
        if k:
            to_pair[k].wait_recv()
            r.o2send[k - 1] = (kept[k] + orecv[k].astype(F32)).astype(BF16)
            to_out[k] = remote(r.o2send.at[k - 1], r.o2recv.at[k - 1], r.sems.out, k - 1, y_peer[k])

    to_pair[0].wait_recv()
    result = query_state[...].astype(F32) + kept[0] + orecv[0].astype(F32)
    for k in range(1, chips):
        to_out[k].wait_recv()
        result = result + r.o2recv[k - 1].astype(F32)
    r.cross_out[...] = result.astype(BF16)

    for copy in sends:
        copy.wait_send()


def spread(h, vit_ctx, vit_resid, vit_proj, vit_grad, norm_gain, cross_q, key_w, value_w, out_w, query_state):
    tokens, vrows = vit_ctx.shape
    queries, wide = query_state.shape
    width = vit_proj.shape[2]
    chips, half = h // 2, tokens // 2
    src = dict(
        proj=lax.all_gather(vit_proj, "dp", axis=1, tiled=True)[0], ctx=vit_ctx, grad=vit_grad.T, resid=vit_resid.T,
        key_w=key_w, value_w=value_w, gain=norm_gain, cross_q=cross_q, query_state=query_state, out_w=out_w,
    )
    outs = dict(cross_out=((queries, wide), BF16), ctx_grad=((tokens, vrows), BF16))
    spans = cut(width, 2)
    ahead = max(chips - 1, 1)
    scratch = dict(
        v={k: pltpu.VMEM(a.shape, a.dtype) for k, a in src.items()},
        load=dma(len(src)),
        grad_n=pltpu.VMEM((tokens, width), BF16),
        resid_n=pltpu.VMEM((tokens, width), BF16),
        feat=pltpu.VMEM((tokens, width), BF16),
        osend=pltpu.VMEM((chips, queries, wide), BF16),
        orecv=pltpu.VMEM((chips, queries, wide), BF16),
        kept=pltpu.VMEM((chips, queries, wide), F32),
        o2send=pltpu.VMEM((ahead, queries, wide), BF16),
        o2recv=pltpu.VMEM((ahead, queries, wide), BF16),
        hs=[pltpu.VMEM((2, half, hi - lo), F32) for lo, hi in spans],
        crecv=[pltpu.VMEM((half, hi - lo), F32) for lo, hi in spans],
        ysend=[pltpu.VMEM((half, hi - lo), BF16) for lo, hi in spans],
        yrecv=[pltpu.VMEM((ahead, half, hi - lo), BF16) for lo, hi in spans],
        sems=dict(
            feat=pair(1), pair=pair(chips), out=pair(chips - 1), core=[pair(1) for _ in spans],
            y=[pair(chips - 1) for _ in spans],
        ),
    )
    cross_out, ctx_grad = call(spread_kernel, (h, spans), dict(src=src), outs, scratch)
    proj_grad = lax.psum_scatter(
        lax.dot_general(vit_ctx, vit_grad, (((0,), (0,)), ((), ())), preferred_element_type=F32),
        "dp", scatter_dimension=0, tiled=True,
    )
    return ctx_grad, cross_out, proj_grad


def hand_over_kernel(*refs):
    count, sems = len(refs) // 2, refs[-1]
    copies = [
        pltpu.make_async_copy(src, dst, sems.at[at])
        for at, (src, dst) in enumerate(zip(refs[:count], refs[count:-1]))
    ]
    for copy in copies:
        copy.start()
    for copy in copies:
        copy.wait()


def hand_over(results):
    return pl.pallas_call(
        hand_over_kernel,
        out_shape=[jax.ShapeDtypeStruct(a.shape, a.dtype) for a in results],
        in_specs=[pl.BlockSpec(memory_space=pltpu.VMEM)] * len(results),
        out_specs=[pl.BlockSpec(memory_space=pl.ANY)] * len(results),
        scratch_shapes=[dma(len(results))],
    )(*[pltpu.with_memory_space_constraint(a, pltpu.VMEM) for a in results])


def on_device(
    n, h, vit_ctx, vit_resid, vit_proj, vit_grad, norm_gain, cross_q, key_w, value_w, out_w, query_state
):
    rest = vit_grad, norm_gain, cross_q, key_w, value_w, out_w, query_state
    rows, width = vit_proj.shape[1:]
    if h == 4 and n == 8 and rows % 16 == 0 and width % 32 == 0:
        ctx_grad, cross_out, proj_grad = paired(n, vit_ctx, vit_resid, vit_proj[0], *rest)
    else:
        ctx_grad, cross_out, proj_grad = spread(h, vit_ctx, vit_resid, vit_proj, *rest)
    return ctx_grad, proj_grad[None], cross_out[None]


def solution(mesh):
    return jax.shard_map(
        functools.partial(on_device, mesh.shape["dp"], mesh.shape["head"]),
        mesh=mesh,
        in_specs=(
            P("dp", "head"),
            P("dp", None),
            P("head", "dp", None),
            P("dp", None),
            P(),
            P(None, "head"),
            P(None, "head"),
            P(None, "head"),
            P("head", None),
            P(None, "head"),
        ),
        out_specs=(P("dp", "head"), P("head", "dp", None), P("dp", None, "head")),
        check_vma=False,
    )
```

```python
import functools
import math
from types import SimpleNamespace

import jax
import jax.numpy as jnp
from jax import lax
from jax.experimental import pallas as pl
from jax.experimental.pallas import tpu as pltpu
from jax.sharding import PartitionSpec as P

HD = 128
EPSILON = 1e-06
MESH = pl.DeviceIdType.MESH
F32 = jnp.float32
BF16 = jnp.bfloat16


def named(tree):
    if isinstance(tree, dict):
        return SimpleNamespace(**{k: named(v) for k, v in tree.items()})
    return tree


def remote_in(sends):
    def remote(src, dst, sems, at, device):
        copy = pltpu.make_async_remote_copy(
            src_ref=src,
            dst_ref=dst,
            send_sem=sems[0].at[at],
            recv_sem=sems[1].at[at],
            device_id=device,
            device_id_type=MESH,
        )
        copy.start()
        sends.append(copy)
        return copy

    return remote


def attention(cross_q, keys, values):
    scale = 1.0 / math.sqrt(HD)
    attended = []
    for lo in range(0, keys.shape[1], HD):
        scores = (
            lax.dot_general(
                cross_q[:, lo : lo + HD],
                keys[:, lo : lo + HD],
                (((1,), (1,)), ((), ())),
                preferred_element_type=F32,
            )
            * scale
        )
        exponent = jnp.exp(scores - jnp.max(scores, axis=1, keepdims=True))
        probs = (exponent / jnp.sum(exponent, axis=1, keepdims=True)).astype(BF16)
        attended.append(
            jnp.dot(probs, values[:, lo : lo + HD], preferred_element_type=F32).astype(BF16)
        )
    return jnp.concatenate(attended, axis=1)


def paired_kernel(tree, n, spans, cuts, *refs):
    ins, outs, scratch = jax.tree.unflatten(tree, refs)
    r = named(ins | outs | scratch)
    sends = []
    remote = remote_in(sends)
    d, e = lax.axis_index("dp"), lax.axis_index("head")
    m = n // 2
    z, x = d // 2, lax.rem(d, 2)
    y, c = e // 2, lax.rem(e, 2)
    z_near, z_far = z + 1 - 2 * lax.rem(z, 2), lax.rem(z + 2, m)
    z_last = m - 1 - z
    near, far = (2 * z_near + x, e), (2 * z_far + x, e)
    x_peer, core_peer = (2 * z + 1 - x, e), (d, 2 * y + 1 - c)
    y_peer = (d, 2 * (1 - y) + c)

    greet = [x_peer, core_peer, y_peer, near, far]
    barrier = pltpu.get_barrier_semaphore()
    for device in greet:
        pl.semaphore_signal(barrier, inc=1, device_id=device, device_id_type=MESH)

    proj, gradt = r.src.proj, r.gradt
    rows, width = proj.shape
    tokens = r.v.ctx.shape[0]
    half = tokens // 2
    own, theirs = slice(0, tokens), slice(tokens, 2 * tokens)
    loads = [(r.src.ctx, r.v.ctx)]
    loads += [(proj.at[:, lo:hi], r.gath[i].at[z]) for i, (lo, hi) in enumerate(spans)]
    loads += [(r.src.grad, gradt.at[:, own])]
    streams = [k for k in vars(r.v) if k != "ctx"]
    loads += [(getattr(r.src, k), getattr(r.v, k)) for k in streams]
    loads = [pltpu.make_async_copy(*pair, r.load.at[at]) for at, pair in enumerate(loads)]
    for load in loads:
        load.start()
    first = loads[: 2 + len(spans)]
    waits = named(dict(zip(streams, loads[len(first) :])))

    first[0].wait()
    ctx_all, ctx_t = r.ctx_all, r.ctx_t
    ctx_all[...] = r.v.ctx[...].T.reshape(n, rows, tokens)
    for k in range(m):
        at = slice(k * rows, (k + 1) * rows)
        r.ctx_send[at] = ctx_all[2 * k + 1 - x]
        ctx_t[at, own] = ctx_all[2 * k + x]
    for load in first[1:]:
        load.wait()

    pl.semaphore_wait(barrier, len(greet))
    gather = {}
    to_ctx = remote(r.ctx_send, ctx_t.at[:, theirs], r.sems.ctx, 0, x_peer)

    def gather_own(i, k):
        here = r.gath[i].at[z]
        gather[i, k] = remote(here, here, r.sems.ag[i], k, (far, near)[k])

    ahead, lead, waited = 3, 1, []
    for i in range(len(spans)):
        if i >= ahead:
            gather[i - ahead, 0].wait_send()
            waited.append(gather[i - ahead, 0])
        gather_own(i, 0)
        if i < lead:
            gather_own(i, 1)
        if i == 0:
            part = pl.ds(pl.multiple_of(c * (width // 2), 16), width // 2)
            to_grad = remote(gradt.at[part, own], gradt.at[part, theirs], r.sems.grad, 0, x_peer)

    own_rows = pl.ds(pl.multiple_of(c * half, half), half)
    peer_rows = pl.ds(pl.multiple_of((1 - c) * half, half), half)
    waits.resid.wait()
    resid = r.resid_n
    for lo in range(0, width, 128):
        hi = min(lo + 128, width)
        resid[:, lo:hi] = r.v.resid[lo:hi, :].T

    ctx_n, lhs = r.ctx_n, r.lhs
    to_ctx.wait_recv()
    for at, group in enumerate((own, theirs)):
        ctx_n[at] = ctx_t[:, group].T
        lhs[at * half : (at + 1) * half] = ctx_n[at, peer_rows]
        lhs[(2 + at) * half : (3 + at) * half] = ctx_n[at, own_rows]

    def matrix(i):
        lo, hi = spans[i]
        return r.gath[i][...].reshape(m * rows, hi - lo)

    to_core, to_x, to_y = {}, {}, {}

    def forward(i):
        gather[i, 0].wait_recv()
        here = r.gath[i].at[z_far]
        gather[i, 2] = remote(here, here, r.sems.ag[i], 2, near)

    def product(i):
        gather[i, 1].wait_recv()
        gather[i, 2].wait_recv()
        hs = r.hs[i]
        sums = jnp.dot(lhs[...], matrix(i), preferred_element_type=F32)
        r.csend[i][...] = sums[: 2 * half].astype(BF16)
        to_core[i] = remote(r.csend[i], r.crecv[i], r.sems.core[i], 0, core_peer)
        hs[2 * half :] = sums[2 * half :]

    def exchange(i):
        hs, crecv, psend, precv = r.hs[i], r.crecv[i], r.psend[i], r.precv[i]
        to_core[i].wait_recv()
        if i in y_first:
            chip_sums = hs[2 * half :] + crecv[...].astype(F32)
            hs[2 * half :] = chip_sums
            psend[:2] = chip_sums.astype(BF16).reshape(2, half, hs.shape[1])
            to_y[i] = remote(psend.at[:2], precv.at[:2], r.sems.part[i], 0, y_peer)
            return
        psend[1] = (hs[3 * half :] + crecv[half:].astype(F32)).astype(BF16)
        to_x[i] = remote(psend.at[1], precv.at[1], r.sems.part[i], 1, x_peer)
        chip_sum = hs[2 * half : 3 * half] + crecv[:half].astype(F32)
        hs[2 * half : 3 * half] = chip_sum

    def pass_pair_sum(i):
        hs, psend, precv = r.hs[i], r.psend[i], r.precv[i]
        if i in y_first:
            to_y[i].wait_recv()
            psend[2] = (hs[3 * half :] + precv[1].astype(F32)).astype(BF16)
            to_x[i] = remote(psend.at[2], precv.at[2], r.sems.part[i], 1, x_peer)
            hs[2 * half : 3 * half] = hs[2 * half : 3 * half] + precv[0].astype(F32)
            return
        to_x[i].wait_recv()
        pair_sum = hs[2 * half : 3 * half] + precv[1].astype(F32)
        hs[2 * half : 3 * half] = pair_sum
        psend[0] = pair_sum.astype(BF16)
        to_y[i] = remote(psend.at[0], precv.at[0], r.sems.part[i], 0, y_peer)

    def pass_grad():
        to_grad.wait_recv()
        got = gradt.at[part, theirs]
        return remote(got, got, r.sems.grad, 1, core_peer)

    def weight_grad():
        dwf, zsend = r.dwf, r.zsend
        for lo in range(0, width, 256):
            hi = min(lo + 256, width)
            dwf[:, :, lo:hi] = lax.dot_general(
                ctx_t[...], gradt[lo:hi, :], (((1,), (1,)), ((), ())), preferred_element_type=F32
            ).reshape(m, rows, hi - lo)
        for k, block in enumerate((z_last, z_near)):
            zsend[k] = dwf[block].astype(BF16)

    def pass_weight_grad():
        to_near[0].wait_recv()
        r.zsend[2] = (r.dwf[z_far] + r.zrecv[0].astype(F32)).astype(BF16)
        return remote(r.zsend.at[2], r.zrecv.at[2], r.sems.rs, 2, far)

    last = len(spans) - 1
    y_first, late = (1,), 2
    for i in range(last + 1):
        forward(i)
        if i + lead <= last:
            gather_own(i + lead, 1)
    for i in range(last + 1):
        product(i)
        if i == 0:
            to_grad2 = pass_grad()
        else:
            exchange(i - 1)
        if i == late:
            to_grad2.wait_recv()
            weight_grad()
    to_near = [remote(r.zsend.at[0], r.zrecv.at[0], r.sems.rs, 0, near)]
    exchange(last)
    for i in range(last + 1):
        pass_pair_sum(i)

    grads = 0.0
    for i, (lo, hi) in enumerate(spans):
        grads = grads + jnp.dot(matrix(i), gradt[lo:hi, :], preferred_element_type=F32)
    r.cg_own[...] = grads[:, own].astype(BF16).reshape(m, rows, tokens)
    r.cg_send[...] = grads[:, theirs].astype(BF16).reshape(m, rows, tokens)
    to_cg = remote(r.cg_send, r.cg_recv, r.sems.cg, 0, x_peer)

    to_far = pass_weight_grad()
    to_near.append(remote(r.zsend.at[1], r.zrecv.at[1], r.sems.rs, 1, near))

    feat = r.feat
    total, squares = 0.0, 0.0
    for i, (lo, hi) in enumerate(spans):
        precv, hs = r.precv[i], r.hs[i]
        hidden = resid[own_rows, lo:hi].astype(F32) + hs[2 * half : 3 * half]
        copy, at = (to_x[i], 2) if i in y_first else (to_y[i], 0)
        copy.wait_recv()
        hidden = hidden + precv[at].astype(F32)
        hs[2 * half : 3 * half] = hidden
        total = total + jnp.sum(hidden, axis=1, keepdims=True)
        squares = squares + jnp.sum(hidden * hidden, axis=1, keepdims=True)
    row_mean, square_mean = total / width, squares / width
    variance = square_mean - row_mean * row_mean
    inverse = lax.rsqrt(variance + EPSILON)
    waits.gain.wait()
    scales = r.v.gain[...].reshape(1, width)
    for i, (lo, hi) in enumerate(spans):
        feat[own_rows, lo:hi] = (
            (r.hs[i][2 * half : 3 * half] - row_mean) * inverse * scales[:, lo:hi]
        ).astype(BF16)
    to_feat = remote(feat.at[own_rows], feat.at[own_rows], r.sems.feat, 0, core_peer)
    for load in (waits.key_w, waits.value_w, waits.cross_q):
        load.wait()
    to_feat.wait_recv()

    keys = jnp.dot(feat[...], r.v.key_w[...], preferred_element_type=F32).astype(BF16)
    values = jnp.dot(feat[...], r.v.value_w[...], preferred_element_type=F32).astype(BF16)
    attended = attention(r.v.cross_q, keys, values)

    waits.out_w.wait()
    waits.query_state.wait()
    out_w, query_state = r.v.out_w, r.v.query_state
    wide = query_state.shape[1]

    def term(chip, core, lo, hi):
        at = pl.multiple_of((2 * chip + core) * wide + lo, 128)
        return jnp.dot(attended, out_w[:, pl.ds(at, hi - lo)], preferred_element_type=F32)

    osend, orecv, kept, o2send, o2recv = r.osend, r.orecv, r.kept, r.o2send, r.o2recv
    to_pair, to_out = {}, {}
    for k, chip in ((1, 1 - y), (0, y)):
        for j, (lo, hi) in enumerate(cuts):
            osend[k, :, lo:hi] = term(chip, 1 - c, lo, hi).astype(BF16)
            to_pair[k, j] = remote(
                osend.at[k, :, lo:hi], orecv.at[k, :, lo:hi], r.sems.pair, k * len(cuts) + j, core_peer
            )
        if k:
            for lo, hi in cuts:
                kept[k, :, lo:hi] = term(chip, c, lo, hi)
    for j, (lo, hi) in enumerate(cuts):
        to_pair[1, j].wait_recv()
        o2send[:, lo:hi] = (kept[1, :, lo:hi] + orecv[1, :, lo:hi].astype(F32)).astype(BF16)
        to_out[j] = remote(o2send.at[:, lo:hi], o2recv.at[:, lo:hi], r.sems.out, j, y_peer)
    for j, (lo, hi) in enumerate(cuts):
        to_pair[0, j].wait_recv()
        kept[0, :, lo:hi] = (
            query_state[:, lo:hi].astype(F32) + term(y, c, lo, hi) + orecv[0, :, lo:hi].astype(F32)
        )

    to_cg.wait_recv()
    cg_all = r.cg_all
    for k in range(m):
        cg_all[2 * k + x] = r.cg_own[k]
        cg_all[2 * k + 1 - x] = r.cg_recv[k]
    r.ctx_grad[...] = cg_all[...].reshape(n * rows, tokens).T

    total = r.dwf[z]
    for copy, k in ((to_near[1], 1), (to_far, 2)):
        copy.wait_recv()
        total = total + r.zrecv[k].astype(F32)
    r.proj_grad[...] = total

    for j, (lo, hi) in enumerate(cuts):
        to_out[j].wait_recv()
        r.cross_out[:, lo:hi] = (kept[0, :, lo:hi] + o2recv[:, lo:hi].astype(F32)).astype(BF16)

    for copy in sends:
        if not any(copy is done for done in waited):
            copy.wait_send()


def dma(count):
    return pltpu.SemaphoreType.DMA((max(count, 1),))


def pair(count):
    return dma(count), dma(count)


def call(kernel, sizes, ins, outs, scratch):
    specs, tree = jax.tree.flatten((ins, {k: k for k in outs}, scratch))
    args = jax.tree.leaves(ins)
    results = pl.pallas_call(
        functools.partial(kernel, tree, *sizes),
        out_shape=[pltpu.VMEM(*v) for v in outs.values()],
        in_specs=[pl.BlockSpec(memory_space=pl.ANY)] * len(args),
        out_specs=[pl.BlockSpec(memory_space=pltpu.VMEM)] * len(outs),
        scratch_shapes=specs[len(args) + len(outs) :],
        compiler_params=pltpu.CompilerParams(collective_id=0, has_side_effects=True),
    )(*args)
    return hand_over(results)


def cut(width, parts):
    tiles, spans, at = -(-width // 128), [], 0
    for left in range(parts, 0, -1):
        take = -(-tiles // left) if left > 1 else tiles
        tiles -= take
        spans.append((at, min(at + take * 128, width)))
        at += take * 128
    return spans


def paired(n, vit_ctx, vit_resid, proj, vit_grad, norm_gain, cross_q, key_w, value_w, out_w, query_state):
    rows, width = proj.shape
    tokens, vrows = vit_ctx.shape
    queries, wide = query_state.shape
    m, half = n // 2, tokens // 2
    src = dict(
        proj=proj, ctx=vit_ctx, grad=vit_grad.T, resid=vit_resid.T, key_w=key_w, value_w=value_w,
        gain=norm_gain, cross_q=cross_q, query_state=query_state, out_w=out_w,
    )
    outs = dict(
        cross_out=((queries, wide), BF16), ctx_grad=((tokens, vrows), BF16), proj_grad=((rows, width), F32)
    )
    spans = cut(width, 4)
    cuts = cut(wide, 1)
    direct = dict(proj=proj, grad=vit_grad.T)
    scratch = dict(
        v={k: pltpu.VMEM(a.shape, a.dtype) for k, a in src.items() if k not in direct},
        load=dma(len(src) + len(spans)),
        gradt=pltpu.VMEM((width, 2 * tokens), BF16),
        ctx_all=pltpu.VMEM((n, rows, tokens), BF16),
        ctx_t=pltpu.VMEM((m * rows, 2 * tokens), BF16),
        ctx_send=pltpu.VMEM((m * rows, tokens), BF16),
        ctx_n=pltpu.VMEM((2, tokens, m * rows), BF16),
        lhs=pltpu.VMEM((2 * tokens, m * rows), BF16),
        resid_n=pltpu.VMEM((tokens, width), BF16),
        dwf=pltpu.VMEM((m, rows, width), F32),
        zsend=pltpu.VMEM((m - 1, rows, width), BF16),
        zrecv=pltpu.VMEM((m - 1, rows, width), BF16),
        cg_own=pltpu.VMEM((m, rows, tokens), BF16),
        cg_send=pltpu.VMEM((m, rows, tokens), BF16),
        cg_recv=pltpu.VMEM((m, rows, tokens), BF16),
        cg_all=pltpu.VMEM((n, rows, tokens), BF16),
        feat=pltpu.VMEM((tokens, width), BF16),
        osend=pltpu.VMEM((2, queries, wide), BF16),
        orecv=pltpu.VMEM((2, queries, wide), BF16),
        kept=pltpu.VMEM((2, queries, wide), F32),
        o2send=pltpu.VMEM((queries, wide), BF16),
        o2recv=pltpu.VMEM((queries, wide), BF16),
        gath=[pltpu.VMEM((m, rows, hi - lo), BF16) for lo, hi in spans],
        hs=[pltpu.VMEM((2 * tokens, hi - lo), F32) for lo, hi in spans],
        csend=[pltpu.VMEM((tokens, hi - lo), BF16) for lo, hi in spans],
        crecv=[pltpu.VMEM((tokens, hi - lo), BF16) for lo, hi in spans],
        psend=[pltpu.VMEM((3, half, hi - lo), BF16) for lo, hi in spans],
        precv=[pltpu.VMEM((3, half, hi - lo), BF16) for lo, hi in spans],
        sems=dict(
            ctx=pair(1), grad=pair(2), rs=pair(m - 1), cg=pair(1), feat=pair(1), out=pair(len(cuts)),
            pair=pair(2 * len(cuts)), ag=[pair(m - 1) for _ in spans], core=[pair(1) for _ in spans],
            part=[pair(2) for _ in spans],
        ),
    )
    cross_out, ctx_grad, proj_grad = call(paired_kernel, (n, spans, cuts), dict(src=src), outs, scratch)
    return ctx_grad, cross_out, proj_grad


def spread_kernel(tree, h, spans, *refs):
    ins, outs, scratch = jax.tree.unflatten(tree, refs)
    r = named(ins | outs | scratch)
    sends = []
    remote = remote_in(sends)
    ctx, resid, grad, gain, cross_q, query_state = (
        r.v.ctx, r.v.resid, r.v.grad, r.v.gain, r.v.cross_q, r.v.query_state
    )
    proj = r.v.proj
    d, e = lax.axis_index("dp"), lax.axis_index("head")
    chips = h // 2
    y, c = e // 2, lax.rem(e, 2)
    core_peer = (d, 2 * y + 1 - c)
    y_pos = [y] + [lax.rem(y + k, chips) for k in range(1, chips)]
    y_peer = [(d, 2 * p + c) for p in y_pos]

    waits = {}
    for i, name in enumerate(vars(r.src)):
        waits[name] = pltpu.make_async_copy(getattr(r.src, name), getattr(r.v, name), r.load.at[i])
        waits[name].start()
    waits = named(waits)

    greet = [core_peer] + y_peer[1:]
    greeted = [core_peer] + [(d, 2 * lax.rem(y + chips - k, chips) + c) for k in range(1, chips)]
    barrier = pltpu.get_barrier_semaphore()
    for device in greeted:
        pl.semaphore_signal(barrier, inc=1, device_id=device, device_id_type=MESH)
    pl.semaphore_wait(barrier, len(greet))

    width = spans[-1][1]

    def flip(src, dst):
        for lo in range(0, width, 128):
            hi = min(lo + 128, width)
            dst[:, lo:hi] = src[lo:hi, :].T

    for load in (waits.ctx, waits.grad, waits.resid, waits.proj):
        load.wait()
    flip(grad, r.grad_n)
    flip(resid, r.resid_n)
    grad, resid = r.grad_n, r.resid_n

    half = ctx.shape[0] // 2
    own_rows = pl.ds(pl.multiple_of(c * half, half), half)
    peer_rows = pl.ds(pl.multiple_of((1 - c) * half, half), half)
    feat = r.feat
    to_core, to_y = {}, {}
    for i, (lo, hi) in enumerate(spans):
        hs, ysend, yrecv = r.hs[i], r.ysend[i], r.yrecv[i]
        hs[1] = jnp.dot(ctx[peer_rows, :], proj[:, lo:hi], preferred_element_type=F32)
        to_core[i] = remote(hs.at[1], r.crecv[i], r.sems.core[i], 0, core_peer)
        hs[0] = jnp.dot(ctx[own_rows, :], proj[:, lo:hi], preferred_element_type=F32)
        to_core[i].wait_recv()
        chip_sum = hs[0] + r.crecv[i][...]
        hs[0] = chip_sum
        ysend[...] = chip_sum.astype(BF16)
        for k in range(1, chips):
            to_y[i, k] = remote(ysend, yrecv.at[k - 1], r.sems.y[i], k - 1, y_peer[k])

    grads = 0.0
    for i, (lo, hi) in enumerate(spans):
        grads = grads + lax.dot_general(
            grad[:, lo:hi], proj[:, lo:hi], (((1,), (1,)), ((), ())), preferred_element_type=F32
        )
    r.ctx_grad[...] = grads.astype(BF16)

    total, squares = 0.0, 0.0
    for i, (lo, hi) in enumerate(spans):
        hidden = resid[own_rows, lo:hi].astype(F32) + r.hs[i][0]
        for k in range(1, chips):
            to_y[i, k].wait_recv()
            hidden = hidden + r.yrecv[i][k - 1].astype(F32)
        r.hs[i][0] = hidden
        total = total + jnp.sum(hidden, axis=1, keepdims=True)
        squares = squares + jnp.sum(hidden * hidden, axis=1, keepdims=True)
    row_mean, square_mean = total / width, squares / width
    variance = square_mean - row_mean * row_mean
    inverse = lax.rsqrt(variance + EPSILON)
    waits.gain.wait()
    scales = gain[...].reshape(1, width)
    for i, (lo, hi) in enumerate(spans):
        feat[own_rows, lo:hi] = (
            (r.hs[i][0] - row_mean) * inverse * scales[:, lo:hi]
        ).astype(BF16)
    to_feat = remote(feat.at[own_rows], feat.at[own_rows], r.sems.feat, 0, core_peer)
    for load in (waits.key_w, waits.value_w, waits.cross_q):
        load.wait()
    to_feat.wait_recv()

    keys = jnp.dot(feat[...], r.v.key_w[...], preferred_element_type=F32).astype(BF16)
    values = jnp.dot(feat[...], r.v.value_w[...], preferred_element_type=F32).astype(BF16)
    attended = attention(cross_q, keys, values)

    waits.out_w.wait()
    waits.query_state.wait()
    out_w, wide = r.v.out_w, query_state.shape[1]

    def term(chip, core):
        at = pl.multiple_of((2 * chip + core) * wide, 128)
        return jnp.dot(attended, out_w[:, pl.ds(at, wide)], preferred_element_type=F32)

    osend, orecv, kept = r.osend, r.orecv, r.kept
    to_pair, to_out = {}, {}
    for k in list(range(1, chips)) + [0]:
        osend[k] = term(y_pos[k], 1 - c).astype(BF16)
        to_pair[k] = remote(osend.at[k], orecv.at[k], r.sems.pair, k, core_peer)
        kept[k] = term(y_pos[k], c)
        if k:
            to_pair[k].wait_recv()
            r.o2send[k - 1] = (kept[k] + orecv[k].astype(F32)).astype(BF16)
            to_out[k] = remote(r.o2send.at[k - 1], r.o2recv.at[k - 1], r.sems.out, k - 1, y_peer[k])

    to_pair[0].wait_recv()
    result = query_state[...].astype(F32) + kept[0] + orecv[0].astype(F32)
    for k in range(1, chips):
        to_out[k].wait_recv()
        result = result + r.o2recv[k - 1].astype(F32)
    r.cross_out[...] = result.astype(BF16)

    for copy in sends:
        copy.wait_send()


def spread(h, vit_ctx, vit_resid, vit_proj, vit_grad, norm_gain, cross_q, key_w, value_w, out_w, query_state):
    tokens, vrows = vit_ctx.shape
    queries, wide = query_state.shape
    width = vit_proj.shape[2]
    chips, half = h // 2, tokens // 2
    src = dict(
        proj=lax.all_gather(vit_proj, "dp", axis=1, tiled=True)[0], ctx=vit_ctx, grad=vit_grad.T, resid=vit_resid.T,
        key_w=key_w, value_w=value_w, gain=norm_gain, cross_q=cross_q, query_state=query_state, out_w=out_w,
    )
    outs = dict(cross_out=((queries, wide), BF16), ctx_grad=((tokens, vrows), BF16))
    spans = cut(width, 2)
    ahead = max(chips - 1, 1)
    scratch = dict(
        v={k: pltpu.VMEM(a.shape, a.dtype) for k, a in src.items()},
        load=dma(len(src)),
        grad_n=pltpu.VMEM((tokens, width), BF16),
        resid_n=pltpu.VMEM((tokens, width), BF16),
        feat=pltpu.VMEM((tokens, width), BF16),
        osend=pltpu.VMEM((chips, queries, wide), BF16),
        orecv=pltpu.VMEM((chips, queries, wide), BF16),
        kept=pltpu.VMEM((chips, queries, wide), F32),
        o2send=pltpu.VMEM((ahead, queries, wide), BF16),
        o2recv=pltpu.VMEM((ahead, queries, wide), BF16),
        hs=[pltpu.VMEM((2, half, hi - lo), F32) for lo, hi in spans],
        crecv=[pltpu.VMEM((half, hi - lo), F32) for lo, hi in spans],
        ysend=[pltpu.VMEM((half, hi - lo), BF16) for lo, hi in spans],
        yrecv=[pltpu.VMEM((ahead, half, hi - lo), BF16) for lo, hi in spans],
        sems=dict(
            feat=pair(1), pair=pair(chips), out=pair(chips - 1), core=[pair(1) for _ in spans],
            y=[pair(chips - 1) for _ in spans],
        ),
    )
    cross_out, ctx_grad = call(spread_kernel, (h, spans), dict(src=src), outs, scratch)
    proj_grad = lax.psum_scatter(
        lax.dot_general(vit_ctx, vit_grad, (((0,), (0,)), ((), ())), preferred_element_type=F32),
        "dp", scatter_dimension=0, tiled=True,
    )
    return ctx_grad, cross_out, proj_grad


def hand_over_kernel(*refs):
    count, sems = len(refs) // 2, refs[-1]
    copies = [
        pltpu.make_async_copy(src, dst, sems.at[at])
        for at, (src, dst) in enumerate(zip(refs[:count], refs[count:-1]))
    ]
    for copy in copies:
        copy.start()
    for copy in copies:
        copy.wait()


def hand_over(results):
    return pl.pallas_call(
        hand_over_kernel,
        out_shape=[jax.ShapeDtypeStruct(a.shape, a.dtype) for a in results],
        in_specs=[pl.BlockSpec(memory_space=pltpu.VMEM)] * len(results),
        out_specs=[pl.BlockSpec(memory_space=pl.ANY)] * len(results),
        scratch_shapes=[dma(len(results))],
    )(*[pltpu.with_memory_space_constraint(a, pltpu.VMEM) for a in results])


def on_device(
    n, h, vit_ctx, vit_resid, vit_proj, vit_grad, norm_gain, cross_q, key_w, value_w, out_w, query_state
):
    rest = vit_grad, norm_gain, cross_q, key_w, value_w, out_w, query_state
    rows, width = vit_proj.shape[1:]
    if h == 4 and n == 8 and rows % 16 == 0 and width % 32 == 0:
        ctx_grad, cross_out, proj_grad = paired(n, vit_ctx, vit_resid, vit_proj[0], *rest)
    else:
        ctx_grad, cross_out, proj_grad = spread(h, vit_ctx, vit_resid, vit_proj, *rest)
    return ctx_grad, proj_grad[None], cross_out[None]


def solution(mesh):
    return jax.shard_map(
        functools.partial(on_device, mesh.shape["dp"], mesh.shape["head"]),
        mesh=mesh,
        in_specs=(
            P("dp", "head"),
            P("dp", None),
            P("head", "dp", None),
            P("dp", None),
            P(),
            P(None, "head"),
            P(None, "head"),
            P(None, "head"),
            P("head", None),
            P(None, "head"),
        ),
        out_specs=(P("dp", "head"), P("head", "dp", None), P("dp", None, "head")),
        check_vma=False,
    )
```
